32 devices in a mesh: freq: 8 (over z, y), tm: 4 (over x, core).
Axes of the slice: x: 2, y: 2, z: 4, core: 2. Of those that a mesh axis runs over, the one named last changes fastest.
Arguments:
- voltages: float32 [8, 2, 32, 16384], P('freq', None, None, 'tm'), as said below
- local_delay: int32 [128, 32], P('freq'), may hold values from 0 to 15
- merge_table: int32 [3, 3, 128], P(None, None, 'freq'), may hold values from 0 to 32, as said below
- box_widths: int32 [4], replicated, may hold values from 1 to 32, as said below
Outputs:
- detection: float32 [128, 4, 16384], P('freq', None, 'tm')
The draws below stay inside these ranges and needn't reach their ends.
Inputs may be any that keep to these rules, and one draw needn't show every extreme that they name: `voltages`: finite real and imaginary parts. `merge_table`: for each level l and each band's 16 output trials, entries 0 and 1 are each a permutation of 0 .. 15; entry 2 lies in 0 .. 8 * 2^l and equals that bound for some trial of every level. `box_widths`: the last width is 32.
All inputs are finite; a program needn't handle non-finite values.
Results may differ from the reference program's by a relative error of at most 0.0001.
Values sent between devices are 32-bit elements; how exact they have to be, the bound alone decides.
No kernel may reach another device: no remote copies, remote signals or barrier semaphores. Data moves between devices by JAX's collectives and lax.ppermute only.
A program may use at most 64 MiB of HBM per device.

```python
import math
import jax
import jax.numpy as jnp
from jax import lax

CH_DEV = 32
TAPS = 4
ROWS = 16
LOCAL_MAX = 16
SHIFT_UNIT = 8
NBOX = 4
WMAX = 32
COARSE = 8
DMS = 128
TIMES = 16384
LEVELS = 3


def draw_voltages(key, part):
    shape_all = (COARSE, 2, CH_DEV, TIMES)
    noise_key, gain_key = jax.random.split(key, 2)
    frame_pos = jnp.arange(TIMES, dtype=jnp.float32) / TIMES
    noise_draw = jax.random.normal(noise_key, shape_all, jnp.float32)
    envelope = 3.0 ** frame_pos
    band_gains = jnp.exp(jax.random.uniform(gain_key, (COARSE, 1, 1, 1), jnp.float32, 0.0, 2.302585))
    return noise_draw * jnp.sqrt(envelope) * band_gains


def draw_merge_table(key, part):
    first_key, second_key, third_key = jax.random.split(key, 3)
    ranks = jnp.arange(ROWS, dtype=jnp.int32)

    def scramble(level_key):
        scores = jax.random.randint(level_key, (LEVELS, 1, COARSE, ROWS), 0, 1 << 20) * ROWS + ranks
        return jnp.argsort(scores, axis=-1).astype(jnp.int32).reshape(LEVELS, 1, DMS)
    ceilings = jnp.left_shift(jnp.int32(SHIFT_UNIT), jnp.arange(LEVELS, dtype=jnp.int32)).reshape(LEVELS, 1, 1)
    shifts = jax.random.randint(third_key, (LEVELS, 1, DMS), 0, ceilings + 1)
    shifts = shifts.at[:, :, 0].set(ceilings[:, :, 0])
    return jnp.concatenate([scramble(first_key), scramble(second_key), shifts.astype(jnp.int32)], axis=1)


def draw_box_widths(key, part):
    widths = jax.random.randint(key, (NBOX,), 1, WMAX + 1)
    return widths.at[NBOX - 1].set(WMAX).astype(jnp.int32)


def set_ends(values, rng, low, largest):
    dims = values.shape
    spot = [jax.random.randint(jax.random.fold_in(rng, axis), (), 0, dims[axis]) for axis in range(len(dims))]
    values = values.at[tuple(spot)].set(low)
    longest = dims.index(max(dims))
    spot[longest] = (spot[longest] + 1) % dims[longest]
    return values.at[tuple(spot)].set(largest)


def setup_inputs(seed: int = 0) -> dict:
    key_list = jax.random.split(jax.random.key(seed), 5)
    return {
        "voltages": draw_voltages(jax.random.fold_in(key_list[4], 71), 0),
        "local_delay": set_ends(jax.random.randint(key_list[1], (DMS, CH_DEV), 0, LOCAL_MAX), jax.random.fold_in(key_list[1], 1), 0, LOCAL_MAX - 1).astype(jnp.int32),
        "merge_table": draw_merge_table(jax.random.fold_in(key_list[4], 71), 0),
        "box_widths": draw_box_widths(jax.random.fold_in(key_list[4], 71), 0),
    }


def window_table(tap_count, branches):
    length = tap_count * branches
    positions = jnp.arange(length, dtype=jnp.float32)
    shaped = jnp.sinc((positions - length / 2 + 0.5) / branches)
    hamming = 0.54 - 0.46 * jnp.cos(2.0 * jnp.pi * positions / (length - 1))
    return (shaped * hamming).reshape(tap_count, branches)

def fourier_table(branches):
    column = jnp.arange(branches, dtype=jnp.int32)
    angle = 2.0 * jnp.pi * (column[:, None] * column[None, :] % branches).astype(jnp.float32) / branches
    cosine = jnp.cos(angle)
    sine = jnp.sin(angle)
    upper_half = jnp.concatenate([cosine, sine], axis=1)
    lower_half = jnp.concatenate([-sine, cosine], axis=1)
    return jnp.concatenate([upper_half, lower_half], axis=0)

def reference(voltages, local_delay, merge_table, box_widths):
    band_count = voltages.shape[0]
    time_count = voltages.shape[3]
    window = window_table(TAPS, CH_DEV)
    padded = jnp.pad(voltages, ((0, 0), (0, 0), (0, 0), (TAPS - 1, 0)))
    filtered = jnp.zeros(voltages.shape, jnp.float32)
    for tap_index in range(TAPS):
        filtered = filtered + window[tap_index][None, None, :, None] * padded[:, :, :, tap_index:tap_index + time_count]
    stacked = filtered.reshape(band_count, 2 * CH_DEV, time_count)
    spectra = jnp.einsum('ij,fjt->fit', fourier_table(CH_DEV), stacked, precision=lax.Precision.HIGHEST)
    intensity = spectra[:, :CH_DEV] ** 2 + spectra[:, CH_DEV:] ** 2
    band_mean = lax.optimization_barrier(jnp.sum(intensity, axis=2, keepdims=True)) / time_count
    normed = intensity / (band_mean + 1e-06) - 1.0
    delays = local_delay.reshape(band_count, ROWS, CH_DEV)
    widened = jnp.pad(normed, ((0, 0), (0, 0), (LOCAL_MAX - 1, 0)))
    dm_rows = jnp.zeros((band_count, ROWS, time_count), jnp.float32)
    for lag_index in range(LOCAL_MAX):
        selector = (delays == lag_index).astype(jnp.float32)
        lagged = widened[:, :, LOCAL_MAX - 1 - lag_index:LOCAL_MAX - 1 - lag_index + time_count]
        dm_rows = dm_rows + jnp.einsum('frc,fct->frt', selector, lagged, precision=lax.Precision.HIGHEST)
    band_index = jnp.arange(band_count, dtype=jnp.int32)
    for level_index in range(LEVELS):
        stride = 2 ** level_index
        delay_reach = SHIFT_UNIT * stride
        lower_band = band_index - band_index // stride % 2 * stride
        upper_band = lower_band + stride
        level_table = merge_table[level_index].reshape(3, band_count, ROWS)
        picked_low = jax.vmap(lambda block, chosen: block[chosen])(dm_rows[lower_band], level_table[0])
        picked_high = jax.vmap(lambda block, chosen: block[chosen])(dm_rows[upper_band], level_table[1])
        padded_high = jnp.pad(picked_high, ((0, 0), (0, 0), (delay_reach, 0))).reshape(band_count * ROWS, delay_reach + time_count)
        starts = (delay_reach - level_table[2].reshape(-1)).astype(jnp.int32)
        delayed = jax.vmap(lambda one_row, row_start: lax.dynamic_slice_in_dim(one_row, row_start, time_count))(padded_high, starts)
        dm_rows = picked_low + delayed.reshape(band_count, ROWS, time_count)
    dedispersed = dm_rows.reshape(band_count * ROWS, time_count) / math.sqrt(band_count * CH_DEV)
    widened_dm = jnp.pad(dedispersed, ((0, 0), (WMAX - 1, 0)))
    detection = jnp.zeros((band_count * ROWS, NBOX, time_count), jnp.float32)
    for offset in range(WMAX):
        width_mask = (offset < box_widths).astype(jnp.float32)
        lagged = widened_dm[:, WMAX - 1 - offset:WMAX - 1 - offset + time_count]
        detection = detection + lagged[:, None, :] * width_mask[None, :, None]
    return detection / jnp.sqrt(box_widths.astype(jnp.float32))[None, :, None]
```

```python
import functools
import math

import jax
import jax.numpy as jnp
import numpy as np
from jax import lax
from jax.experimental import pallas as pl
from jax.experimental.pallas import tpu as pltpu
from jax.sharding import PartitionSpec as P

TAPS = 4
LOCAL_MAX = 16
SHIFT_UNIT = 8
WMAX = 32
LANES = 128
SPREAD = 3

epsilon = 1e-06

VM = pl.BlockSpec(memory_space=pltpu.VMEM)
SM = pl.BlockSpec(memory_space=pltpu.SMEM)
F32 = jnp.float32
BF16 = jnp.bfloat16


def swapped(value, axis, mask):
    pairs = [(source, source ^ mask) for source in range(lax.axis_size(axis))]
    return lax.ppermute(value, axis, pairs)


def shifted(block, axis, distance):
    devices = range(lax.axis_size(axis))
    route = [(i - distance, i) for i in devices if i - distance in devices]
    return lax.ppermute(block, axis, route)


def window_table(branches):
    length = TAPS * branches
    positions = np.arange(length, dtype=np.float64)
    shaped = np.sinc((positions - length / 2 + 0.5) / branches)
    hamming = 0.54 - 0.46 * np.cos(2.0 * np.pi * positions / (length - 1))
    return (shaped * hamming).reshape(TAPS, branches).astype(np.float32)


def fourier_table(branches):
    column = np.arange(branches)
    angle = 2.0 * np.pi * (column[:, None] * column[None, :] % branches) / branches
    cosine = np.cos(angle)
    sine = np.sin(angle)
    upper_half = np.concatenate([cosine, sine], axis=1)
    lower_half = np.concatenate([-sine, cosine], axis=1)
    return np.concatenate([upper_half, lower_half], axis=0).astype(np.float32)


def halves(x):
    high = x.astype(BF16)
    return high, (x - high.astype(F32)).astype(BF16)


def thirds(x):
    high = x.astype(BF16)
    rest = x - high.astype(F32)
    middle = rest.astype(BF16)
    return high, middle, (rest - middle.astype(F32)).astype(BF16)


def lane_index(shape):
    return lax.broadcasted_iota(jnp.int32, shape, len(shape) - 1)


def row_index(shape):
    return lax.broadcasted_iota(jnp.int32, shape, 0)


def channel_kernel(
    x_ref, win_ref, w_ref, power_ref, small_ref, big_ref, carry_ref, acc_ref, own_ref
):
    step = pl.program_id(0)
    rows, width = x_ref.shape
    branches = rows // 2

    @pl.when(step == 0)
    def _():
        carry_ref[...] = jnp.zeros_like(carry_ref)
        acc_ref[...] = jnp.zeros_like(acc_ref)

    def spectra_of(extended):
        filtered = win_ref[:, TAPS - 1 : TAPS] * extended[:, LANES:]
        for back in range(1, TAPS):
            moved = pltpu.roll(extended, back, 1)[:, LANES:]
            filtered = filtered + win_ref[:, TAPS - 1 - back : TAPS - back] * moved
        high, low = halves(filtered)
        stack = jnp.concatenate([high, low, high, low], axis=0)
        return jnp.dot(w_ref[...], stack, preferred_element_type=F32)

    x = x_ref[...]
    spectra = spectra_of(jnp.concatenate([carry_ref[...], x], axis=1))
    power = spectra[:branches] ** 2 + spectra[branches:] ** 2
    power_ref[...] = power
    first = power[:, :LANES]
    keep = (lane_index(first.shape) >= TAPS - 1) | (step > 0)
    total = acc_ref[...] + jnp.where(keep, first, 0.0)
    for tile in range(1, width // LANES):
        total = total + power[:, tile * LANES : (tile + 1) * LANES]
    acc_ref[...] = total
    carry_ref[...] = x[:, width - LANES :]

    @pl.when(step == 0)
    def _():
        own_ref[...] = spectra[:, :LANES]

    @pl.when(step == pl.num_programs(0) - 1)
    def _():
        last = carry_ref[...]
        following = spectra_of(jnp.concatenate([last, jnp.zeros_like(last)], axis=1))
        sums = jnp.sum(acc_ref[...], axis=1, keepdims=True)
        sums = jnp.concatenate([sums, jnp.zeros_like(sums)], axis=0)
        lane = lane_index((rows, LANES))
        edge = TAPS - 1
        packed = jnp.where(lane == 2 * edge, sums, 0.0)
        packed = jnp.where(lane < 2 * edge, pltpu.roll(own_ref[...], edge, 1), packed)
        packed = jnp.where(lane < edge, following, packed)
        packed = jnp.concatenate([packed, jnp.zeros((LANES - rows, LANES), F32)], axis=0)
        packet = jnp.transpose(packed)[:8]
        small_ref[...] = packet
        big_ref[:8] = packet
        big_ref[8:] = power[:, width - LANES :]


def channelize(samples, block):
    rows, time_count = samples.shape
    branches = rows // 2
    window = window_table(branches)
    columns = np.zeros((rows, LANES), np.float32)
    columns[:, :TAPS] = np.concatenate([window, window], axis=1).T
    table = jnp.asarray(fourier_table(branches))
    high, low = halves(table)
    weights = jnp.concatenate([high, high, low, low], axis=1)
    return pl.pallas_call(
        channel_kernel,
        grid=(time_count // block,),
        in_specs=[
            pl.BlockSpec((rows, block), lambda i: (0, i)),
            pl.BlockSpec((rows, LANES), lambda i: (0, 0)),
            pl.BlockSpec((rows, 4 * rows), lambda i: (0, 0)),
        ],
        out_specs=[
            pl.BlockSpec((branches, block), lambda i: (0, i)),
            pl.BlockSpec((8, LANES), lambda i: (0, 0)),
            pl.BlockSpec((8 + branches, LANES), lambda i: (0, 0)),
        ],
        out_shape=[
            jax.ShapeDtypeStruct((branches, time_count), F32),
            jax.ShapeDtypeStruct((8, LANES), F32),
            jax.ShapeDtypeStruct((8 + branches, LANES), F32),
        ],
        scratch_shapes=[
            pltpu.VMEM((rows, LANES), F32),
            pltpu.VMEM((branches, LANES), F32),
            pltpu.VMEM((rows, LANES), F32),
        ],
        compiler_params=pltpu.CompilerParams(vmem_limit_bytes=16 << 20),
        name="channelize",
    )(samples, jnp.asarray(columns), weights)


def local_kernel(peers, chunks, time_all, block, *refs):
    power_ref, packets = refs[0], refs[1 : 1 + peers]
    delay_ref, table_ref = refs[1 + peers : 3 + peers]
    outs = refs[3 + peers : 3 + peers + chunks]
    line_ref, fold_ref, rows_ref = refs[3 + peers + chunks :]
    branches, time_count = power_ref.shape
    trials = delay_ref.shape[0]
    rank = lax.axis_index("tm")
    band = lax.axis_index("freq")
    edge = TAPS - 1

    line_ref[:8] = jnp.zeros((8, LANES), F32)
    for peer in range(peers):
        spot = pl.multiple_of(((rank ^ peer) + 1) * 8, 8)
        line_ref[pl.ds(spot, 8), :] = packets[peer][:8]
    mine = line_ref[8:]
    amplitude = mine + pltpu.roll(line_ref[: 8 * peers], edge, 0)
    square = amplitude * amplitude
    folded = square + pltpu.roll(square, LANES - branches, 1)
    fold_ref[...] = folded
    kind = row_index(mine.shape) % 8
    whole = jnp.where(kind == 2 * edge, mine, 0.0)
    whole = jnp.where((kind >= edge) & (kind < 2 * edge), folded, whole)
    band_mean = jnp.sum(whole, axis=0, keepdims=True) / time_all
    scale = 1.0 / (band_mean + epsilon)
    firsts = fold_ref[pl.ds(pl.multiple_of(rank * 8, 8), 8), :]
    firsts = jnp.where(row_index(firsts.shape) == 2 * edge, scale, firsts)
    columns = jnp.transpose(firsts)[:branches]
    scale = columns[:, 2 * edge : 2 * edge + 1]

    tail = jnp.zeros((branches, LANES), F32)
    for peer in range(1, peers):
        if peer & (peer + 1) == 0:
            tail = jnp.where((rank ^ (rank - 1)) == peer, packets[peer][8:], tail)
    halo = jnp.where(rank > 0, tail * scale - 1.0, 0.0)
    start = power_ref[:, :LANES]
    for lane in range(edge):
        value = columns[:, edge + lane : edge + lane + 1]
        start = jnp.where(lane_index(start.shape) == lane, value, start)

    fine, parts = 2, 3
    depth = fine * parts * branches
    spread = row_index((branches, depth)) == lane_index((branches, depth)) % branches
    wanted = jnp.dot(
        delay_ref[...].astype(BF16), spread.astype(BF16), preferred_element_type=F32
    ).astype(jnp.int32)
    offset = lane_index((trials, depth)) // (parts * branches)
    coarse = LOCAL_MAX // fine
    selector = jnp.concatenate(
        [(wanted == offset + fine * step).astype(F32) for step in range(coarse)], axis=0
    ).astype(BF16)

    def trial_rows(value, value_before, products_before):
        joined = jnp.concatenate([value_before, value], axis=1)
        stack = []
        for lag in range(fine):
            moved = pltpu.roll(joined, lag, 1)[:, LANES:] if lag else value
            stack.extend(thirds(moved))
        products = jnp.dot(
            selector, jnp.concatenate(stack, axis=0), preferred_element_type=F32
        )
        rows = products[:trials]
        for step in range(1, coarse):
            part = slice(step * trials, (step + 1) * trials)
            both = jnp.concatenate([products_before[part], products[part]], axis=1)
            rows = rows + pltpu.roll(both, fine * step, 1)[:, LANES:]
        width = value.shape[1]
        return rows, value[:, width - LANES :], products[:, width - LANES :]

    nothing = jnp.zeros((coarse * trials, LANES), F32)
    rows, value_before, products_before = trial_rows(halo, jnp.zeros_like(halo), nothing)
    rows_ref[:, :LANES] = rows

    def some(index, carried):
        spot = pl.multiple_of(index * block, block)
        value = power_ref[:, pl.ds(spot, block)]
        head = jnp.where(index == 0, start, value[:, :LANES])
        value = jnp.concatenate([head, value[:, LANES:]], axis=1)
        rows, *carried = trial_rows(value * scale - 1.0, *carried)
        rows_ref[:, pl.ds(pl.multiple_of(spot + LANES, LANES), block)] = rows
        return tuple(carried)

    lax.fori_loop(0, time_count // block, some, (value_before, products_before))

    chunk = time_count // chunks
    entries = table_ref.shape[1]
    table = table_ref[...]
    for peer in range(chunks):
        spot = pl.multiple_of(((band ^ peer) & (chunks - 1)) * chunk, LANES)
        head = rows_ref[:, pl.ds(spot, LANES)]
        outs[peer][:, :LANES] = jnp.where(lane_index(head.shape) < entries_used(chunks), table, head)
        outs[peer][:, LANES:] = rows_ref[:, pl.ds(pl.multiple_of(spot + LANES, LANES), chunk)]


def entries_used(chunks):
    return 3 * (chunks.bit_length() - 1)


def local_rows(power, packets, delays, table, chunks, time_all):
    branches, time_count = power.shape
    trials = delays.shape[0]
    peers = len(packets)
    shape = jax.ShapeDtypeStruct((trials, LANES + time_count // chunks), F32)
    return pl.pallas_call(
        functools.partial(local_kernel, peers, chunks, time_all, 512),
        in_specs=[VM] * (3 + peers),
        out_specs=[VM] * chunks,
        out_shape=[shape] * chunks,
        scratch_shapes=[
            pltpu.VMEM((8 * (peers + 1), LANES), F32),
            pltpu.VMEM((8 * peers, LANES), F32),
            pltpu.VMEM((trials, LANES + time_count), F32),
        ],
        compiler_params=pltpu.CompilerParams(vmem_limit_bytes=16 << 20),
        name="local_rows",
    )(power, *packets, delays, table)


def merge_kernel(chunks, *refs):
    ins, outs = refs[:chunks], refs[chunks:]
    trials = ins[0].shape[0]
    count = chunks * trials
    band = lax.axis_index("freq")
    rows = jnp.concatenate([ref[...] for ref in ins], axis=0)
    table = rows[:, :LANES].astype(jnp.int32)
    place = row_index((count, count)) // trials
    column = lane_index((count, count))
    for level in range(chunks.bit_length() - 1):
        reach = SHIFT_UNIT << level
        upper = ((place ^ band) >> level) & 1
        low_place = place ^ (upper << level)
        high_place = low_place ^ (1 << level)
        low = table[:, 3 * level : 3 * level + 1] + low_place * trials
        high = table[:, 3 * level + 1 : 3 * level + 2] + high_place * trials
        pick = jnp.concatenate([column == low, column == high], axis=0).astype(F32).astype(BF16)
        pick = jnp.concatenate([pick] * 3, axis=1)
        stack = jnp.concatenate(thirds(rows), axis=0)
        picked = jnp.dot(pick, stack, preferred_element_type=F32)
        delayed = picked[count:]
        amount = table[:, 3 * level + 2 : 3 * level + 3]
        for bit in range(reach.bit_length()):
            moved = pltpu.roll(delayed, 1 << bit, 1)
            delayed = jnp.where(((amount >> bit) & 1) == 1, moved, delayed)
        rows = picked[:count] + delayed
    for peer in range(chunks):
        outs[peer][...] = rows[peer * trials : (peer + 1) * trials]


def merged_chunks(pieces):
    chunks = len(pieces)
    shape = jax.ShapeDtypeStruct(pieces[0].shape, F32)
    return pl.pallas_call(
        functools.partial(merge_kernel, chunks),
        in_specs=[VM] * chunks,
        out_specs=[VM] * chunks,
        out_shape=[shape] * chunks,
        compiler_params=pltpu.CompilerParams(vmem_limit_bytes=16 << 20),
        name="merge",
    )(*pieces)


def boxcar_kernel(chunks, divisor, width_ref, *refs):
    ins, out_ref, line_ref, mask_ref = refs[:chunks], *refs[chunks:]
    trials, boxes, width = out_ref.shape
    step = pl.program_id(0)
    band = lax.axis_index("freq")
    chunk = ins[0].shape[1] - LANES

    @pl.when(step == 0)
    def _():
        for peer in range(chunks):
            index = (band ^ peer) & (chunks - 1)
            spot = pl.multiple_of(index * chunk + LANES, LANES)
            line_ref[:, pl.ds(spot, chunk)] = ins[peer][:, LANES:]

            @pl.when(index == 0)
            def _():
                line_ref[:, :LANES] = ins[peer][:, :LANES]

        shape = (2 * LANES, LANES)
        back = lane_index(shape) + LANES - row_index(shape)
        for box in range(boxes):
            inside = (back >= 0) & (back < width_ref[box])
            mask_ref[:, box * LANES : (box + 1) * LANES] = inside.astype(F32).astype(BF16)

    base = pl.multiple_of(step * width, LANES)
    tiles = width // LANES
    pairs = [
        line_ref[:, pl.ds(pl.multiple_of(base + tile * LANES, LANES), 2 * LANES)]
        for tile in range(tiles)
    ]
    high, low = halves(jnp.concatenate(pairs, axis=0))
    mask = mask_ref[...]
    sums = jnp.dot(high, mask, preferred_element_type=F32) + jnp.dot(
        low, mask, preferred_element_type=F32
    )
    for box in range(boxes):
        wide = jnp.full((1, LANES), width_ref[box], jnp.int32).astype(F32)
        factor = 1.0 / (jnp.sqrt(wide) * divisor)
        for tile in range(tiles):
            part = sums[tile * trials : (tile + 1) * trials, box * LANES : (box + 1) * LANES]
            out_ref[:, box, tile * LANES : (tile + 1) * LANES] = part * factor


def boxcars(pieces, widths, divisor, block):
    chunks = len(pieces)
    trials = pieces[0].shape[0]
    time_count = (pieces[0].shape[1] - LANES) * chunks
    boxes = widths.shape[0]
    whole = pl.BlockSpec(pieces[0].shape, lambda i: (0, 0))
    return pl.pallas_call(
        functools.partial(boxcar_kernel, chunks, divisor),
        grid=(time_count // block,),
        in_specs=[SM] + [whole] * chunks,
        out_specs=pl.BlockSpec((trials, boxes, block), lambda i: (0, 0, i)),
        out_shape=jax.ShapeDtypeStruct((trials, boxes, time_count), F32),
        scratch_shapes=[
            pltpu.VMEM((trials, LANES + time_count), F32),
            pltpu.VMEM((2 * LANES, boxes * LANES), BF16),
        ],
        compiler_params=pltpu.CompilerParams(vmem_limit_bytes=16 << 20),
        name="boxcar",
    )(widths, *pieces)


def selector_rows(chosen, row_count):
    return (chosen[:, None] == jnp.arange(row_count, dtype=jnp.int32)[None, :]).astype(F32)


def delay_rows(picked_high, delay_amount, delay_reach):
    current = picked_high
    for bit_index in range(delay_reach.bit_length()):
        step_size = 2**bit_index
        moved = jnp.concatenate(
            [
                jnp.zeros((current.shape[0], step_size), F32),
                current[:, : current.shape[1] - step_size],
            ],
            axis=1,
        )
        bit_set = (jnp.right_shift(delay_amount, bit_index) % 2 == 1)[:, None]
        current = jnp.where(bit_set, moved, current)
    return current[:, delay_reach:]


def merge_level(own_rows, their_rows, level_table, is_upper, delay_reach):
    lower_rows = jnp.where(is_upper, their_rows, own_rows)
    upper_rows = jnp.where(is_upper, own_rows, their_rows)
    row_count = own_rows.shape[0]
    pick = functools.partial(jnp.dot, precision=lax.Precision.HIGHEST, preferred_element_type=F32)
    picked_low = pick(selector_rows(level_table[0], row_count), lower_rows[:, delay_reach:])
    picked_high = pick(selector_rows(level_table[1], row_count), upper_rows)
    return picked_low + delay_rows(picked_high, level_table[2], delay_reach)


def boxcar(dedispersed, widths):
    time_count = dedispersed.shape[1] - (WMAX - 1)
    detection = jnp.zeros((dedispersed.shape[0], widths.shape[0], time_count), F32)
    for offset in range(WMAX):
        width_mask = (offset < widths).astype(F32)
        lagged = dedispersed[:, WMAX - 1 - offset : WMAX - 1 - offset + time_count]
        detection = detection + lagged[:, None, :] * width_mask[None, :, None]
    return detection / jnp.sqrt(widths.astype(F32))[None, :, None]


def body(voltages, local_delay, merge_table, box_widths):
    branches = voltages.shape[2]
    time_count = voltages.shape[3]
    freq_size = lax.axis_size("freq")
    tm_size = lax.axis_size("tm")
    level_count = freq_size.bit_length() - 1
    spread_levels = min(SPREAD, level_count)
    chunks = 2**spread_levels
    trials = local_delay.shape[0]

    power, small, big = channelize(voltages.reshape(2 * branches, time_count), 1024)
    packets = [small]
    for peer in range(1, tm_size):
        packets.append(swapped(big if peer & (peer + 1) == 0 else small, "tm", peer))

    entries = merge_table[:spread_levels].reshape(3 * spread_levels, trials).T.astype(F32)
    entries = jnp.pad(entries, ((0, 0), (0, LANES - 3 * spread_levels)))
    pieces = local_rows(
        power, packets, local_delay, entries, chunks, float(time_count * tm_size)
    )
    pieces = [piece if p == 0 else swapped(piece, "freq", p) for p, piece in enumerate(pieces)]
    pieces = merged_chunks(pieces)
    pieces = [piece if p == 0 else swapped(piece, "freq", p) for p, piece in enumerate(pieces)]
    divisor = math.sqrt(branches * freq_size)
    if level_count == spread_levels:
        return boxcars(pieces, box_widths, divisor, 1024)

    freq_rank = lax.axis_index("freq")
    order = jnp.arange(chunks, dtype=jnp.int32) ^ (freq_rank & (chunks - 1))
    stacked = jnp.stack([piece[:, LANES:] for piece in pieces])[order]
    dm_rows = jnp.transpose(stacked, (1, 0, 2)).reshape(trials, time_count)
    for level_index in range(spread_levels, level_count):
        delay_reach = SHIFT_UNIT * 2**level_index
        tail_rows = shifted(dm_rows[:, time_count - delay_reach :], "tm", 1)
        own_rows = jnp.concatenate([tail_rows, dm_rows], axis=1)
        their_rows = swapped(own_rows, "freq", 2**level_index)
        is_upper = jnp.right_shift(freq_rank, level_index) % 2 == 1
        dm_rows = merge_level(own_rows, their_rows, merge_table[level_index], is_upper, delay_reach)
    tail_rows = shifted(dm_rows[:, time_count - (WMAX - 1) :], "tm", 1)
    return boxcar(jnp.concatenate([tail_rows, dm_rows], axis=1) / divisor, box_widths)


def solution(mesh):
    return jax.shard_map(
        body,
        mesh=mesh,
        in_specs=(P("freq", None, None, "tm"), P("freq", None), P(None, None, "freq"), P()),
        out_specs=P("freq", None, "tm"),
        check_vma=False,
    )
```

```python
import functools
import math

import jax
import jax.numpy as jnp
import numpy as np
from jax import lax
from jax.experimental import pallas as pl
from jax.experimental.pallas import tpu as pltpu
from jax.sharding import PartitionSpec as P

TAPS = 4
LOCAL_MAX = 16
SHIFT_UNIT = 8
WMAX = 32
LANES = 128
STREAMED = 3

epsilon = 1e-06

VM = pl.BlockSpec(memory_space=pltpu.VMEM)
SM = pl.BlockSpec(memory_space=pltpu.SMEM)
HBM = pl.BlockSpec(memory_space=pltpu.HBM)
PARAMS = pltpu.CompilerParams(vmem_limit_bytes=16 << 20)
F32 = jnp.float32
BF16 = jnp.bfloat16


def swapped(value, axis, mask):
    pairs = [(source, source ^ mask) for source in range(lax.axis_size(axis))]
    return lax.ppermute(value, axis, pairs)


def shifted(block, axis, distance):
    devices = range(lax.axis_size(axis))
    route = [(i - distance, i) for i in devices if i - distance in devices]
    return lax.ppermute(block, axis, route)


def window_table(branches):
    length = TAPS * branches
    positions = np.arange(length, dtype=np.float64)
    shaped = np.sinc((positions - length / 2 + 0.5) / branches)
    hamming = 0.54 - 0.46 * np.cos(2.0 * np.pi * positions / (length - 1))
    return (shaped * hamming).reshape(TAPS, branches).astype(np.float32)


def fourier_table(branches):
    column = np.arange(branches)
    angle = 2.0 * np.pi * (column[:, None] * column[None, :] % branches) / branches
    cosine = np.cos(angle)
    sine = np.sin(angle)
    upper_half = np.concatenate([cosine, sine], axis=1)
    lower_half = np.concatenate([-sine, cosine], axis=1)
    return np.concatenate([upper_half, lower_half], axis=0).astype(np.float32)


def halves(x):
    high = x.astype(BF16)
    return high, (x - high.astype(F32)).astype(BF16)


def thirds(x):
    high = x.astype(BF16)
    rest = x - high.astype(F32)
    middle = rest.astype(BF16)
    return high, middle, (rest - middle.astype(F32)).astype(BF16)


def lane_index(shape):
    return lax.broadcasted_iota(jnp.int32, shape, len(shape) - 1)


def row_index(shape):
    return lax.broadcasted_iota(jnp.int32, shape, 0)


def channel_kernel(
    pieces, x_hbm, win_hbm, w_hbm, power_ref, small_ref, big_ref, x_ref, win_ref, w_ref, sems
):
    rows, time_count = x_ref.shape
    branches = rows // 2
    width = time_count // pieces
    edge = TAPS - 1
    copies = [
        pltpu.make_async_copy(win_hbm, win_ref, sems.at[0]),
        pltpu.make_async_copy(w_hbm, w_ref, sems.at[1]),
    ]
    for piece in range(pieces):
        part = pl.ds(piece * width, width)
        copies.append(
            pltpu.make_async_copy(x_hbm.at[:, part], x_ref.at[:, part], sems.at[2 + piece])
        )
    for copy in copies:
        copy.start()
    copies[0].wait()
    copies[1].wait()

    total = jnp.zeros((branches, LANES), F32)
    for piece in range(pieces):
        copies[2 + piece].wait()
        start = piece * width
        here = x_ref[:, start : start + width]
        if piece:
            parts = [x_ref[:, start - LANES : start], here]
        else:
            parts = [jnp.zeros((rows, LANES), F32), here]
        if piece == pieces - 1:
            parts.append(jnp.zeros((rows, LANES), F32))
        extended = jnp.concatenate(parts, axis=1)
        filtered = win_ref[:, edge:TAPS] * extended[:, LANES:]
        for back in range(1, TAPS):
            moved = pltpu.roll(extended, back, 1)[:, LANES:]
            filtered = filtered + win_ref[:, edge - back : TAPS - back] * moved
        high, low = halves(filtered)
        stack = jnp.concatenate([high, low, high, low], axis=0)
        spectra = jnp.dot(w_ref[...], stack, preferred_element_type=F32)
        power = spectra[:branches, :width] ** 2 + spectra[branches:, :width] ** 2
        power_ref[:, start : start + width] = power
        if piece == 0:
            own = spectra[:, :LANES]
        for tile in range(width // LANES):
            value = power[:, tile * LANES : (tile + 1) * LANES]
            if piece == 0 and tile == 0:
                value = jnp.where(lane_index(value.shape) >= edge, value, 0.0)
            total = total + value
    following = spectra[:, width:]
    sums = jnp.sum(total, axis=1, keepdims=True)
    sums = jnp.concatenate([sums, jnp.zeros_like(sums)], axis=0)
    lane = lane_index((rows, LANES))
    packed = jnp.where(lane == 2 * edge, sums, 0.0)
    packed = jnp.where(lane < 2 * edge, pltpu.roll(own, edge, 1), packed)
    packed = jnp.where(lane < edge, following, packed)
    packed = jnp.concatenate([packed, jnp.zeros((LANES - rows, LANES), F32)], axis=0)
    packet = jnp.transpose(packed)[:8]
    small_ref[...] = packet
    big_ref[:8] = packet
    big_ref[8:] = power[:, width - LANES :]


def channelize(samples, pieces):
    rows, time_count = samples.shape
    branches = rows // 2
    window = window_table(branches)
    columns = np.zeros((rows, LANES), np.float32)
    columns[:, :TAPS] = np.concatenate([window, window], axis=1).T
    table = jnp.asarray(fourier_table(branches))
    high, low = halves(table)
    weights = jnp.concatenate([high, high, low, low], axis=1)
    return pl.pallas_call(
        functools.partial(channel_kernel, pieces),
        in_specs=[HBM] * 3,
        out_specs=[VM] * 3,
        out_shape=[
            jax.ShapeDtypeStruct((branches, time_count), F32),
            jax.ShapeDtypeStruct((8, LANES), F32),
            jax.ShapeDtypeStruct((8 + branches, LANES), F32),
        ],
        scratch_shapes=[
            pltpu.VMEM((rows, time_count), F32),
            pltpu.VMEM((rows, LANES), F32),
            pltpu.VMEM((rows, 4 * rows), BF16),
            pltpu.SemaphoreType.DMA((2 + pieces,)),
        ],
        compiler_params=PARAMS,
        name="channelize",
    )(samples, jnp.asarray(columns), weights)


FINE = 2
PARTS = 3


def trial_rows(selector, trials, value, value_before, products_before):
    joined = jnp.concatenate([value_before, value], axis=1)
    stack = []
    for lag in range(FINE):
        moved = pltpu.roll(joined, lag, 1)[:, LANES:] if lag else value
        stack.extend(thirds(moved))
    products = jnp.dot(selector, jnp.concatenate(stack, axis=0), preferred_element_type=F32)
    rows = products[:trials]
    for step in range(1, LOCAL_MAX // FINE):
        part = slice(step * trials, (step + 1) * trials)
        both = jnp.concatenate([products_before[part], products[part]], axis=1)
        rows = rows + pltpu.roll(both, FINE * step, 1)[:, LANES:]
    width = value.shape[1]
    return rows, value[:, width - LANES :], products[:, width - LANES :]


def first_rows_kernel(peers, time_all, *refs):
    power_ref, packets, delay_ref = refs[0], refs[1 : 1 + peers], refs[1 + peers]
    rows_ref, scale_ref, selector_ref, line_ref, fold_ref = refs[2 + peers :]
    branches = power_ref.shape[0]
    trials = delay_ref.shape[0]
    rank = lax.axis_index("tm")
    edge = TAPS - 1

    line_ref[:8] = jnp.zeros((8, LANES), F32)
    for peer in range(peers):
        spot = pl.multiple_of(((rank ^ peer) + 1) * 8, 8)
        line_ref[pl.ds(spot, 8), :] = packets[peer][:8]
    mine = line_ref[8:]
    amplitude = mine + pltpu.roll(line_ref[: 8 * peers], edge, 0)
    square = amplitude * amplitude
    folded = square + pltpu.roll(square, LANES - branches, 1)
    fold_ref[...] = folded
    kind = row_index(mine.shape) % 8
    whole = jnp.where(kind == 2 * edge, mine, 0.0)
    whole = jnp.where((kind >= edge) & (kind < 2 * edge), folded, whole)
    band_mean = jnp.sum(whole, axis=0, keepdims=True) / time_all
    scale = 1.0 / (band_mean + epsilon)
    firsts = fold_ref[pl.ds(pl.multiple_of(rank * 8, 8), 8), :]
    firsts = jnp.where(row_index(firsts.shape) == 2 * edge, scale, firsts)
    columns = jnp.transpose(firsts)[:branches]
    scale = jnp.broadcast_to(columns[:, 2 * edge : 2 * edge + 1], (branches, LANES))
    scale_ref[...] = scale
    scale = scale[:, :1]

    tail = jnp.zeros((branches, LANES), F32)
    for peer in range(1, peers):
        if peer & (peer + 1) == 0:
            tail = jnp.where((rank ^ (rank - 1)) == peer, packets[peer][8:], tail)
    halo = jnp.where(rank > 0, tail * scale - 1.0, 0.0)
    start = power_ref[:, :LANES]
    for lane in range(edge):
        value = columns[:, edge + lane : edge + lane + 1]
        start = jnp.where(lane_index(start.shape) == lane, value, start)

    depth = FINE * PARTS * branches
    spread = row_index((branches, depth)) == lane_index((branches, depth)) % branches
    wanted = jnp.dot(
        delay_ref[...].astype(BF16), spread.astype(BF16), preferred_element_type=F32
    ).astype(jnp.int32)
    offset = lane_index((trials, depth)) // (PARTS * branches)
    coarse = LOCAL_MAX // FINE
    selector = jnp.concatenate(
        [(wanted == offset + FINE * step).astype(F32) for step in range(coarse)], axis=0
    ).astype(BF16)
    selector_ref[...] = selector

    width = rows_ref.shape[1] - LANES
    value = jnp.concatenate([start, power_ref[:, LANES:width]], axis=1) * scale - 1.0
    value = jnp.concatenate([halo, value], axis=1)
    nothing = jnp.zeros((coarse * trials, LANES), F32)
    rows_ref[...], _, _ = trial_rows(selector, trials, value, jnp.zeros_like(halo), nothing)


def first_rows(power, packets, delays, tiles, time_all):
    branches = power.shape[0]
    trials = delays.shape[0]
    peers = len(packets)
    depth = FINE * PARTS * branches
    return pl.pallas_call(
        functools.partial(first_rows_kernel, peers, time_all),
        in_specs=[VM] * (2 + peers),
        out_specs=[VM] * 3,
        out_shape=[
            jax.ShapeDtypeStruct((trials, tiles * LANES), F32),
            jax.ShapeDtypeStruct((branches, LANES), F32),
            jax.ShapeDtypeStruct((LOCAL_MAX // FINE * trials, depth), BF16),
        ],
        scratch_shapes=[
            pltpu.VMEM((8 * (peers + 1), LANES), F32),
            pltpu.VMEM((8 * peers, LANES), F32),
        ],
        compiler_params=PARAMS,
        name="first_rows",
    )(power, *packets, delays)


def more_rows_kernel(start, power_ref, scale_ref, selector_ref, rows_ref):
    trials, width = rows_ref.shape
    scale = scale_ref[:, :1]
    value = power_ref[:, start - LANES : start + width] * scale - 1.0
    selector = selector_ref[...]
    nothing = jnp.zeros((selector.shape[0], LANES), F32)
    rows, _, _ = trial_rows(selector, trials, value, jnp.zeros_like(value[:, :LANES]), nothing)
    rows_ref[...] = rows[:, LANES:]


def more_rows(power, scale, selector, start, tiles):
    trials = selector.shape[0] * FINE // LOCAL_MAX
    return pl.pallas_call(
        functools.partial(more_rows_kernel, start),
        in_specs=[VM] * 3,
        out_specs=VM,
        out_shape=jax.ShapeDtypeStruct((trials, tiles * LANES), F32),
        compiler_params=PARAMS,
        name="more_rows",
    )(power, scale, selector)


def merged(level, first, refs):
    table_ref, own_ref, their_ref = refs[:3]
    trials, width = own_ref.shape
    upper = (lax.axis_index("freq") >> level) & 1
    if first:
        before = jnp.zeros((trials, LANES), F32)
        own = jnp.concatenate([before, own_ref[...]], axis=1)
        their = jnp.concatenate([before, their_ref[...]], axis=1)
    else:
        own = jnp.concatenate([refs[3][:, refs[3].shape[1] - LANES :], own_ref[...]], axis=1)
        their = jnp.concatenate([refs[4][:, refs[4].shape[1] - LANES :], their_ref[...]], axis=1)
    table = table_ref[...].astype(jnp.int32)
    column = lane_index((trials, 2 * trials))
    low = table[:, 3 * level : 3 * level + 1] + upper * trials
    high = table[:, 3 * level + 1 : 3 * level + 2] + (1 - upper) * trials
    pick = jnp.concatenate([column == low, column == high], axis=0).astype(F32).astype(BF16)
    pick = jnp.concatenate([pick] * 3, axis=1)
    stack = jnp.concatenate(thirds(jnp.concatenate([own, their], axis=0)), axis=0)
    picked = jnp.dot(pick, stack, preferred_element_type=F32)
    delayed = picked[trials:]
    amount = table[:, 3 * level + 2 : 3 * level + 3]
    for bit in range((SHIFT_UNIT << level).bit_length()):
        moved = pltpu.roll(delayed, 1 << bit, 1)
        delayed = jnp.where(((amount >> bit) & 1) == 1, moved, delayed)
    return picked[:trials, LANES:] + delayed[:, LANES:]


def merge_kernel(level, first, *refs):
    refs[-1][...] = merged(level, first, refs[:-1])


def merge(level, table, own, their, before):
    return pl.pallas_call(
        functools.partial(merge_kernel, level, not before),
        in_specs=[VM] * (3 + len(before)),
        out_specs=VM,
        out_shape=jax.ShapeDtypeStruct(own.shape, F32),
        compiler_params=PARAMS,
        name="merge",
    )(table, own, their, *before)


def mask_kernel(divisor, width_ref, after_ref, mask_ref, factor_ref):
    del after_ref
    shape = (2 * LANES, LANES)
    back = lane_index(shape) + LANES - row_index(shape)
    boxes = width_ref.shape[0]
    wide = jnp.ones(factor_ref.shape, jnp.int32)
    for box in range(boxes):
        inside = (back >= 0) & (back < width_ref[box])
        mask_ref[:, box * LANES : (box + 1) * LANES] = inside.astype(F32).astype(BF16)
        wide = jnp.where(row_index(wide.shape) == box, width_ref[box], wide)
    factor_ref[...] = 1.0 / (jnp.sqrt(wide.astype(F32)) * divisor)


def box_masks(widths, divisor, after):
    boxes = widths.shape[0]
    return pl.pallas_call(
        functools.partial(mask_kernel, divisor),
        in_specs=[SM, VM],
        out_specs=[VM] * 2,
        out_shape=[
            jax.ShapeDtypeStruct((2 * LANES, boxes * LANES), BF16),
            jax.ShapeDtypeStruct((-(-boxes // 8) * 8, LANES), F32),
        ],
        compiler_params=PARAMS,
        name="box_masks",
    )(widths, after)


def detect_kernel(level, start, *refs):
    first = start == 0
    table_ref, mask_ref, factor_ref, own_ref, their_ref = refs[:5]
    rows_ref, out_hbm, out_ref, sem = refs[-4:]
    rows = merged(level, first, (table_ref, own_ref, their_ref, *refs[5:7]))
    rows_ref[...] = rows
    if not first:
        before = refs[7]
        rows = jnp.concatenate([before[:, before.shape[1] - LANES :], rows], axis=1)
    trials, boxes, width = out_ref.shape
    tiles = width // LANES
    pairs = [rows[:, tile * LANES : (tile + 2) * LANES] for tile in range(tiles)]
    high, low = halves(jnp.concatenate(pairs, axis=0))
    mask = mask_ref[...]
    sums = jnp.dot(high, mask, preferred_element_type=F32) + jnp.dot(
        low, mask, preferred_element_type=F32
    )
    for box in range(boxes):
        factor = factor_ref[box : box + 1]
        for tile in range(tiles):
            part = sums[tile * trials : (tile + 1) * trials, box * LANES : (box + 1) * LANES]
            out_ref[:, box, tile * LANES : (tile + 1) * LANES] = part * factor
    copy = pltpu.make_async_copy(out_ref, out_hbm.at[:, :, pl.ds(start, width)], sem)
    copy.start()
    copy.wait()


def detect(level, start, shape, table, masks, own, their, before, out):
    trials, width = own.shape
    operands = [table, *masks, own, their, *before]
    specs = [VM] * len(operands)
    aliases = {}
    if out is not None:
        aliases = {len(operands): 1}
        operands.append(out)
        specs.append(HBM)
    if start == 0:
        width = width - LANES
    return pl.pallas_call(
        functools.partial(detect_kernel, level, start),
        in_specs=specs,
        out_specs=[VM, HBM],
        out_shape=[jax.ShapeDtypeStruct(own.shape, F32), jax.ShapeDtypeStruct(shape, F32)],
        scratch_shapes=[
            pltpu.VMEM((trials, shape[1], width), F32),
            pltpu.SemaphoreType.DMA,
        ],
        input_output_aliases=aliases,
        compiler_params=PARAMS,
        name="detect",
    )(*operands)


def selector_rows(chosen, row_count):
    return (chosen[:, None] == jnp.arange(row_count, dtype=jnp.int32)[None, :]).astype(F32)


def delay_rows(picked_high, delay_amount, delay_reach):
    current = picked_high
    for bit_index in range(delay_reach.bit_length()):
        step_size = 2**bit_index
        moved = jnp.concatenate(
            [
                jnp.zeros((current.shape[0], step_size), F32),
                current[:, : current.shape[1] - step_size],
            ],
            axis=1,
        )
        bit_set = (jnp.right_shift(delay_amount, bit_index) % 2 == 1)[:, None]
        current = jnp.where(bit_set, moved, current)
    return current[:, delay_reach:]


def merge_level(own_rows, their_rows, level_table, is_upper, delay_reach):
    lower_rows = jnp.where(is_upper, their_rows, own_rows)
    upper_rows = jnp.where(is_upper, own_rows, their_rows)
    row_count = own_rows.shape[0]
    pick = functools.partial(jnp.dot, precision=lax.Precision.HIGHEST, preferred_element_type=F32)
    picked_low = pick(selector_rows(level_table[0], row_count), lower_rows[:, delay_reach:])
    picked_high = pick(selector_rows(level_table[1], row_count), upper_rows)
    return picked_low + delay_rows(picked_high, level_table[2], delay_reach)


def boxcar(dedispersed, widths):
    time_count = dedispersed.shape[1] - (WMAX - 1)
    detection = jnp.zeros((dedispersed.shape[0], widths.shape[0], time_count), F32)
    for offset in range(WMAX):
        width_mask = (offset < widths).astype(F32)
        lagged = dedispersed[:, WMAX - 1 - offset : WMAX - 1 - offset + time_count]
        detection = detection + lagged[:, None, :] * width_mask[None, :, None]
    return detection / jnp.sqrt(widths.astype(F32))[None, :, None]


def body(voltages, local_delay, merge_table, box_widths):
    branches = voltages.shape[2]
    time_count = voltages.shape[3]
    freq_size = lax.axis_size("freq")
    tm_size = lax.axis_size("tm")
    level_count = freq_size.bit_length() - 1
    streamed = min(STREAMED, level_count)
    trials = local_delay.shape[0]
    divisor = math.sqrt(branches * freq_size)

    power, small, big = channelize(voltages.reshape(2 * branches, time_count), 4)
    packets = [small]
    for peer in range(1, tm_size):
        packets.append(swapped(big if peer & (peer + 1) == 0 else small, "tm", peer))

    table = merge_table[:streamed].reshape(3 * streamed, trials).T.astype(F32)
    table = jnp.pad(table, ((0, 0), (0, LANES - 3 * streamed)))
    tiles = 1 + time_count // LANES
    sizes = [3 * tiles // 11, 4 * tiles // 11]
    sizes.append(tiles - sum(sizes))
    starts = [sum(sizes[:i]) * LANES - LANES for i in range(len(sizes))]
    rows, scale, selector = first_rows(
        power, packets, local_delay, sizes[0], float(time_count * tm_size)
    )
    pieces = [rows]
    for start, size in zip(starts[1:], sizes[1:]):
        pieces.append(more_rows(power, scale, selector, start, size))
    masks = box_masks(box_widths, divisor, scale) if level_count == streamed else None

    for level in range(streamed):
        their = [swapped(piece, "freq", 2**level) for piece in pieces]
        results = []
        out = None
        for i, start in enumerate(starts):
            before = [pieces[i - 1], their[i - 1]] if i else []
            if level < level_count - 1:
                results.append(merge(level, table, pieces[i], their[i], before))
                continue
            if i:
                before.append(results[i - 1])
            shape = (trials, box_widths.shape[0], time_count)
            rows, out = detect(
                level, max(start, 0), shape, table, masks, pieces[i], their[i], before, out
            )
            results.append(rows)
        pieces = results
    if level_count == streamed:
        return out

    freq_rank = lax.axis_index("freq")
    dm_rows = jnp.concatenate(pieces, axis=1)[:, LANES:]
    for level_index in range(streamed, level_count):
        delay_reach = SHIFT_UNIT * 2**level_index
        tail_rows = shifted(dm_rows[:, time_count - delay_reach :], "tm", 1)
        own_rows = jnp.concatenate([tail_rows, dm_rows], axis=1)
        their_rows = swapped(own_rows, "freq", 2**level_index)
        is_upper = jnp.right_shift(freq_rank, level_index) % 2 == 1
        dm_rows = merge_level(own_rows, their_rows, merge_table[level_index], is_upper, delay_reach)
    tail_rows = shifted(dm_rows[:, time_count - (WMAX - 1) :], "tm", 1)
    return boxcar(jnp.concatenate([tail_rows, dm_rows], axis=1) / divisor, box_widths)


def solution(mesh):
    return jax.shard_map(
        body,
        mesh=mesh,
        in_specs=(P("freq", None, None, "tm"), P("freq", None), P(None, None, "freq"), P()),
        out_specs=P("freq", None, "tm"),
        check_vma=False,
    )
```

```python
import functools
import math

import jax
import jax.numpy as jnp
from jax import lax
from jax.experimental import pallas as pl
from jax.experimental.pallas import tpu as pltpu
from jax.sharding import PartitionSpec as P

TAPS = 4
LOCAL_MAX = 16
SHIFT_UNIT = 8
WMAX = 32
LANES = 128
OUT_COPIES = 2
PIECES = 3
STREAMED = 3

epsilon = 1e-06

VM = pl.BlockSpec(memory_space=pltpu.VMEM)
SM = pl.BlockSpec(memory_space=pltpu.SMEM)
HBM = pl.BlockSpec(memory_space=pltpu.HBM)
PARAMS = pltpu.CompilerParams(vmem_limit_bytes=16 << 20)
SOURCE_LIMIT = 54_000_000
F32 = jnp.float32
BF16 = jnp.bfloat16


def swapped(value, axis, mask):
    pairs = [(source, source ^ mask) for source in range(lax.axis_size(axis))]
    return lax.ppermute(value, axis, pairs)


def shifted(block, axis, distance):
    devices = range(lax.axis_size(axis))
    route = [(i - distance, i) for i in devices if i - distance in devices]
    return lax.ppermute(block, axis, route)


def window_columns(branches):
    shape = (branches, LANES)
    place = (lane_index(shape) % TAPS * branches + row_index(shape)).astype(F32)
    length = TAPS * branches
    offset = (place - length / 2 + 0.5) * (math.pi / branches)
    hamming = 0.54 - 0.46 * jnp.cos(place * (2.0 * math.pi / (length - 1)))
    return jnp.sin(offset) / offset * hamming


def fourier_rows(branches):
    shape = (2 * branches, 4 * branches)
    row, column = row_index(shape), lane_index(shape)
    quarter = branches // 4
    turn = (row % branches) * (column % branches)
    turn = turn + jnp.where(row >= branches, 2 * quarter, quarter)
    turn = turn - jnp.where(column % (2 * branches) >= branches, quarter, 0)
    turn = turn % branches
    negative = turn > 2 * quarter
    turn = jnp.where(negative, turn - 2 * quarter, turn)
    turn = jnp.where(turn > quarter, 2 * quarter - turn, turn)
    value = jnp.zeros(shape, F32)
    for step in range(1, quarter + 1):
        value = jnp.where(turn == step, math.sin(2.0 * math.pi * step / branches), value)
    return jnp.where(negative, -value, value)


def halves(x):
    high = x.astype(BF16)
    return high, (x - high.astype(F32)).astype(BF16)


def thirds(x):
    high = x.astype(BF16)
    rest = x - high.astype(F32)
    middle = rest.astype(BF16)
    return high, middle, (rest - middle.astype(F32)).astype(BF16)


def lane_index(shape):
    return lax.broadcasted_iota(jnp.int32, shape, len(shape) - 1)


def row_index(shape):
    return lax.broadcasted_iota(jnp.int32, shape, 0)


def channel_kernel(pieces, x_hbm, power_ref, small_ref, big_ref, x_ref, win_ref, w_ref, sems):
    rows, time_count = x_ref.shape
    branches = rows // 2
    width = time_count // pieces
    edge = TAPS - 1
    copies = []
    for piece in range(pieces):
        part = pl.ds(piece * width, width)
        copies.append(pltpu.make_async_copy(x_hbm.at[:, part], x_ref.at[:, part], sems.at[piece]))
        copies[-1].start()
    window = window_columns(branches)
    for half in range(2):
        win_ref[half * branches : (half + 1) * branches] = window
    w_ref[...] = jnp.concatenate(halves(fourier_rows(branches)), axis=1)

    total = jnp.zeros((branches, LANES), F32)
    for piece in range(pieces):
        copies[piece].wait()
        start = piece * width
        here = x_ref[:, start : start + width]
        if piece:
            parts = [x_ref[:, start - LANES : start], here]
        else:
            parts = [jnp.zeros((rows, LANES), F32), here]
        if piece == pieces - 1:
            parts.append(jnp.zeros((rows, LANES), F32))
        extended = jnp.concatenate(parts, axis=1)
        filtered = win_ref[:, edge:TAPS] * extended[:, LANES:]
        for back in range(1, TAPS):
            moved = pltpu.roll(extended, back, 1)[:, LANES:]
            filtered = filtered + win_ref[:, edge - back : TAPS - back] * moved
        high, low = halves(filtered)
        stack = jnp.concatenate([high, low, high, low], axis=0)
        spectra = jnp.dot(w_ref[...], stack, preferred_element_type=F32)
        power = spectra[:branches, :width] ** 2 + spectra[branches:, :width] ** 2
        power_ref[:, start : start + width] = power
        if piece == 0:
            own = spectra[:, :LANES]
        for tile in range(width // LANES):
            value = power[:, tile * LANES : (tile + 1) * LANES]
            if piece == 0 and tile == 0:
                value = jnp.where(lane_index(value.shape) >= edge, value, 0.0)
            total = total + value
    following = spectra[:, width:]
    sums = jnp.sum(total, axis=1, keepdims=True)
    sums = jnp.concatenate([sums, jnp.zeros_like(sums)], axis=0)
    lane = lane_index((rows, LANES))
    packed = jnp.where(lane == 2 * edge, sums, 0.0)
    packed = jnp.where(lane < 2 * edge, pltpu.roll(own, edge, 1), packed)
    packed = jnp.where(lane < edge, following, packed)
    packed = jnp.concatenate([packed, jnp.zeros((LANES - rows, LANES), F32)], axis=0)
    packet = jnp.transpose(packed)[:8]
    small_ref[...] = packet
    big_ref[:8] = packet
    big_ref[8:] = power[:, width - LANES :]


def channelize(samples, pieces):
    rows, time_count = samples.shape
    branches = rows // 2
    return pl.pallas_call(
        functools.partial(channel_kernel, pieces),
        in_specs=[HBM],
        out_specs=[VM] * 3,
        out_shape=[
            jax.ShapeDtypeStruct((branches, time_count), F32),
            jax.ShapeDtypeStruct((8, LANES), F32),
            jax.ShapeDtypeStruct((8 + branches, LANES), F32),
        ],
        scratch_shapes=[
            pltpu.VMEM((rows, time_count), F32),
            pltpu.VMEM((rows, LANES), F32),
            pltpu.VMEM((rows, 4 * rows), BF16),
            pltpu.SemaphoreType.DMA((pieces,)),
        ],
        compiler_params=pltpu.CompilerParams(vmem_limit_bytes=SOURCE_LIMIT),
        name="channelize",
    )(samples)


FINE = 2
PARTS = 3


def trial_rows(selector, trials, value, value_before, products_before):
    joined = jnp.concatenate([value_before, value], axis=1)
    stack = []
    for lag in range(FINE):
        moved = pltpu.roll(joined, lag, 1)[:, LANES:] if lag else value
        stack.extend(thirds(moved))
    products = jnp.dot(selector, jnp.concatenate(stack, axis=0), preferred_element_type=F32)
    rows = products[:trials]
    for step in range(1, LOCAL_MAX // FINE):
        part = slice(step * trials, (step + 1) * trials)
        both = jnp.concatenate([products_before[part], products[part]], axis=1)
        rows = rows + pltpu.roll(both, FINE * step, 1)[:, LANES:]
    width = value.shape[1]
    return rows, value[:, width - LANES :], products[:, width - LANES :]


def first_rows_kernel(peers, time_all, *refs):
    power_ref, packets, delay_ref = refs[0], refs[1 : 1 + peers], refs[1 + peers]
    rows_ref, scale_ref, selector_ref, line_ref, fold_ref = refs[2 + peers :]
    branches = power_ref.shape[0]
    trials = delay_ref.shape[0]
    rank = lax.axis_index("tm")
    edge = TAPS - 1

    line_ref[:8] = jnp.zeros((8, LANES), F32)
    for peer in range(peers):
        spot = pl.multiple_of(((rank ^ peer) + 1) * 8, 8)
        line_ref[pl.ds(spot, 8), :] = packets[peer][:8]
    mine = line_ref[8:]
    amplitude = mine + pltpu.roll(line_ref[: 8 * peers], edge, 0)
    square = amplitude * amplitude
    folded = square + pltpu.roll(square, LANES - branches, 1)
    fold_ref[...] = folded
    kind = row_index(mine.shape) % 8
    whole = jnp.where(kind == 2 * edge, mine, 0.0)
    whole = jnp.where((kind >= edge) & (kind < 2 * edge), folded, whole)
    band_mean = jnp.sum(whole, axis=0, keepdims=True) / time_all
    scale = 1.0 / (band_mean + epsilon)
    firsts = fold_ref[pl.ds(pl.multiple_of(rank * 8, 8), 8), :]
    firsts = jnp.where(row_index(firsts.shape) == 2 * edge, scale, firsts)
    columns = jnp.transpose(firsts)[:branches]
    scale = jnp.broadcast_to(columns[:, 2 * edge : 2 * edge + 1], (branches, LANES))
    scale_ref[...] = scale
    scale = scale[:, :1]

    tail = jnp.zeros((branches, LANES), F32)
    for peer in range(1, peers):
        if peer & (peer + 1) == 0:
            tail = jnp.where((rank ^ (rank - 1)) == peer, packets[peer][8:], tail)
    halo = jnp.where(rank > 0, tail * scale - 1.0, 0.0)
    start = power_ref[:, :LANES]
    for lane in range(edge):
        value = columns[:, edge + lane : edge + lane + 1]
        start = jnp.where(lane_index(start.shape) == lane, value, start)

    depth = FINE * PARTS * branches
    spread = row_index((branches, depth)) == lane_index((branches, depth)) % branches
    wanted = jnp.dot(
        delay_ref[...].astype(BF16), spread.astype(BF16), preferred_element_type=F32
    ).astype(jnp.int32)
    offset = lane_index((trials, depth)) // (PARTS * branches)
    coarse = LOCAL_MAX // FINE
    selector = jnp.concatenate(
        [(wanted == offset + FINE * step).astype(F32) for step in range(coarse)], axis=0
    ).astype(BF16)
    selector_ref[...] = selector

    width = rows_ref.shape[1] - LANES
    value = jnp.concatenate([start, power_ref[:, LANES:width]], axis=1) * scale - 1.0
    value = jnp.concatenate([halo, value], axis=1)
    nothing = jnp.zeros((coarse * trials, LANES), F32)
    rows_ref[...], _, _ = trial_rows(selector, trials, value, jnp.zeros_like(halo), nothing)


def first_rows(power, packets, delays, tiles, time_all):
    branches = power.shape[0]
    trials = delays.shape[0]
    peers = len(packets)
    depth = FINE * PARTS * branches
    return pl.pallas_call(
        functools.partial(first_rows_kernel, peers, time_all),
        in_specs=[VM] * (2 + peers),
        out_specs=[VM] * 3,
        out_shape=[
            jax.ShapeDtypeStruct((trials, tiles * LANES), F32),
            jax.ShapeDtypeStruct((branches, LANES), F32),
            jax.ShapeDtypeStruct((LOCAL_MAX // FINE * trials, depth), BF16),
        ],
        scratch_shapes=[
            pltpu.VMEM((8 * (peers + 1), LANES), F32),
            pltpu.VMEM((8 * peers, LANES), F32),
        ],
        compiler_params=PARAMS,
        name="first_rows",
    )(power, *packets, delays)


def more_rows_kernel(start, power_ref, scale_ref, selector_ref, rows_ref):
    trials, width = rows_ref.shape
    scale = scale_ref[:, :1]
    value = power_ref[:, start - LANES : start + width] * scale - 1.0
    selector = selector_ref[...]
    nothing = jnp.zeros((selector.shape[0], LANES), F32)
    rows, _, _ = trial_rows(selector, trials, value, jnp.zeros_like(value[:, :LANES]), nothing)
    rows_ref[...] = rows[:, LANES:]


def more_rows(power, scale, selector, start, tiles):
    trials = selector.shape[0] * FINE // LOCAL_MAX
    return pl.pallas_call(
        functools.partial(more_rows_kernel, start),
        in_specs=[VM] * 3,
        out_specs=VM,
        out_shape=jax.ShapeDtypeStruct((trials, tiles * LANES), F32),
        compiler_params=PARAMS,
        name="more_rows",
    )(power, scale, selector)


def delayed_rows(rows, count, unit, largest):
    result = rows
    for step in range(1, largest + 1):
        result = jnp.where(count == step, pltpu.roll(rows, step * unit, 1), result)
    return result


def merged(level, first, refs):
    table_ref, own_ref, their_ref = refs[:3]
    trials, _ = own_ref.shape
    upper = (lax.axis_index("freq") >> level) & 1
    if first:
        before = jnp.zeros((trials, LANES), F32)
        own = jnp.concatenate([before, own_ref[...]], axis=1)
        their = jnp.concatenate([before, their_ref[...]], axis=1)
    else:
        own = jnp.concatenate([refs[3][:, refs[3].shape[1] - LANES :], own_ref[...]], axis=1)
        their = jnp.concatenate([refs[4][:, refs[4].shape[1] - LANES :], their_ref[...]], axis=1)
    table = table_ref[...].astype(jnp.int32)
    column = lane_index((trials, 2 * trials))
    low = table[:, 3 * level : 3 * level + 1] + upper * trials
    high = table[:, 3 * level + 1 : 3 * level + 2] + (1 - upper) * trials
    pick = jnp.concatenate([column == low, column == high], axis=0).astype(F32).astype(BF16)
    pick = jnp.concatenate([pick] * 3, axis=1)
    stack = jnp.concatenate(thirds(jnp.concatenate([own, their], axis=0)), axis=0)
    picked = jnp.dot(pick, stack, preferred_element_type=F32)
    delayed = picked[trials:]
    amount = table[:, 3 * level + 2 : 3 * level + 3]
    delayed = delayed_rows(delayed, amount & (SHIFT_UNIT - 1), 1, SHIFT_UNIT - 1)
    delayed = delayed_rows(delayed, amount // SHIFT_UNIT, SHIFT_UNIT, 1 << level)
    return picked[:trials, LANES:] + delayed[:, LANES:]


def merge_kernel(level, first, *refs):
    refs[-1][...] = merged(level, first, refs[:-1])


def merge(level, table, own, their, before):
    return pl.pallas_call(
        functools.partial(merge_kernel, level, not before),
        in_specs=[VM] * (3 + len(before)),
        out_specs=VM,
        out_shape=jax.ShapeDtypeStruct(own.shape, F32),
        compiler_params=PARAMS,
        name="merge",
    )(table, own, their, *before)


def mask_kernel(divisor, width_ref, after_ref, mask_ref, factor_ref):
    del after_ref
    shape = (2 * LANES, LANES)
    back = lane_index(shape) + LANES - row_index(shape)
    boxes = width_ref.shape[0]
    wide = jnp.ones(factor_ref.shape, jnp.int32)
    for box in range(boxes):
        inside = (back >= 0) & (back < width_ref[box])
        mask_ref[:, box * LANES : (box + 1) * LANES] = inside.astype(F32).astype(BF16)
        wide = jnp.where(row_index(wide.shape) == box, width_ref[box], wide)
    factor_ref[...] = 1.0 / (jnp.sqrt(wide.astype(F32)) * divisor)


def box_masks(widths, divisor, after):
    boxes = widths.shape[0]
    return pl.pallas_call(
        functools.partial(mask_kernel, divisor),
        in_specs=[SM, VM],
        out_specs=[VM] * 2,
        out_shape=[
            jax.ShapeDtypeStruct((2 * LANES, boxes * LANES), BF16),
            jax.ShapeDtypeStruct((-(-boxes // 8) * 8, LANES), F32),
        ],
        compiler_params=PARAMS,
        name="box_masks",
    )(widths, after)


def detect_kernel(level, start, *refs):
    first = start == 0
    table_ref, mask_ref, factor_ref, own_ref, their_ref = refs[:5]
    rows_ref, out_hbm, out_ref, sem = refs[-4:]
    rows = merged(level, first, (table_ref, own_ref, their_ref, *refs[5:7]))
    rows_ref[...] = rows
    if not first:
        before = refs[7]
        rows = jnp.concatenate([before[:, before.shape[1] - LANES :], rows], axis=1)
    trials, boxes, width = out_ref.shape
    tiles = width // LANES
    pairs = [rows[:, tile * LANES : (tile + 2) * LANES] for tile in range(tiles)]
    high, low = halves(jnp.concatenate(pairs, axis=0))
    mask = mask_ref[...]
    sums = jnp.dot(high, mask, preferred_element_type=F32) + jnp.dot(
        low, mask, preferred_element_type=F32
    )
    copies = []
    bounds = [tiles * part // OUT_COPIES for part in range(OUT_COPIES + 1)]
    for number, (begin, end) in enumerate(zip(bounds, bounds[1:])):
        for box in range(boxes):
            factor = factor_ref[box : box + 1]
            for tile in range(begin, end):
                part = sums[tile * trials : (tile + 1) * trials, box * LANES : (box + 1) * LANES]
                out_ref[:, box, tile * LANES : (tile + 1) * LANES] = part * factor
        count = (end - begin) * LANES
        copies.append(
            pltpu.make_async_copy(
                out_ref.at[:, :, pl.ds(begin * LANES, count)],
                out_hbm.at[:, :, pl.ds(start + begin * LANES, count)],
                sem.at[number],
            )
        )
        copies[-1].start()
    for copy in copies:
        copy.wait()


def detect(level, start, shape, table, masks, own, their, before, out):
    trials, width = own.shape
    operands = [table, *masks, own, their, *before]
    specs = [VM] * len(operands)
    aliases = {}
    if out is not None:
        aliases = {len(operands): 1}
        operands.append(out)
        specs.append(HBM)
    if start == 0:
        width = width - LANES
    return pl.pallas_call(
        functools.partial(detect_kernel, level, start),
        in_specs=specs,
        out_specs=[VM, HBM],
        out_shape=[jax.ShapeDtypeStruct(own.shape, F32), jax.ShapeDtypeStruct(shape, F32)],
        scratch_shapes=[
            pltpu.VMEM((trials, shape[1], width), F32),
            pltpu.SemaphoreType.DMA((OUT_COPIES,)),
        ],
        input_output_aliases=aliases,
        compiler_params=PARAMS,
        name="detect",
    )(*operands)


def selector_rows(chosen, row_count):
    return (chosen[:, None] == jnp.arange(row_count, dtype=jnp.int32)[None, :]).astype(F32)


def delay_rows(picked_high, delay_amount, delay_reach):
    current = picked_high
    for bit_index in range(delay_reach.bit_length()):
        step_size = 2**bit_index
        moved = jnp.concatenate(
            [
                jnp.zeros((current.shape[0], step_size), F32),
                current[:, : current.shape[1] - step_size],
            ],
            axis=1,
        )
        bit_set = (jnp.right_shift(delay_amount, bit_index) % 2 == 1)[:, None]
        current = jnp.where(bit_set, moved, current)
    return current[:, delay_reach:]


def merge_level(own_rows, their_rows, level_table, is_upper, delay_reach):
    lower_rows = jnp.where(is_upper, their_rows, own_rows)
    upper_rows = jnp.where(is_upper, own_rows, their_rows)
    row_count = own_rows.shape[0]
    pick = functools.partial(jnp.dot, precision=lax.Precision.HIGHEST, preferred_element_type=F32)
    picked_low = pick(selector_rows(level_table[0], row_count), lower_rows[:, delay_reach:])
    picked_high = pick(selector_rows(level_table[1], row_count), upper_rows)
    return picked_low + delay_rows(picked_high, level_table[2], delay_reach)


def boxcar(dedispersed, widths):
    time_count = dedispersed.shape[1] - (WMAX - 1)
    detection = jnp.zeros((dedispersed.shape[0], widths.shape[0], time_count), F32)
    for offset in range(WMAX):
        width_mask = (offset < widths).astype(F32)
        lagged = dedispersed[:, WMAX - 1 - offset : WMAX - 1 - offset + time_count]
        detection = detection + lagged[:, None, :] * width_mask[None, :, None]
    return detection / jnp.sqrt(widths.astype(F32))[None, :, None]


def body(voltages, local_delay, merge_table, box_widths):
    branches = voltages.shape[2]
    time_count = voltages.shape[3]
    freq_size = lax.axis_size("freq")
    tm_size = lax.axis_size("tm")
    level_count = freq_size.bit_length() - 1
    streamed = min(STREAMED, level_count)
    trials = local_delay.shape[0]
    divisor = math.sqrt(branches * freq_size)

    power, small, big = channelize(voltages.reshape(2 * branches, time_count), 4)
    packets = [small]
    for peer in range(1, tm_size):
        packets.append(swapped(big if peer & (peer + 1) == 0 else small, "tm", peer))

    table = merge_table[:streamed].reshape(3 * streamed, trials).T.astype(F32)
    table = jnp.pad(table, ((0, 0), (0, LANES - 3 * streamed)))
    tiles = 1 + time_count // LANES
    sizes = [3 * tiles // 11, 4 * tiles // 11]
    sizes.append(tiles - sum(sizes))
    starts = [sum(sizes[:i]) * LANES - LANES for i in range(len(sizes))]
    rows, scale, selector = first_rows(
        power, packets, local_delay, sizes[0], float(time_count * tm_size)
    )
    pieces = [rows]
    for i in range(1, PIECES):
        pieces.append(more_rows(power, scale, selector, starts[i], sizes[i]))
    masks = box_masks(box_widths, divisor, scale) if level_count == streamed else None

    for level in range(streamed):
        their = []
        for piece in pieces:
            their.append(swapped(piece, "freq", 2**level))
        results = []
        out = None
        for i, start in enumerate(starts):
            before = [pieces[i - 1], their[i - 1]] if i else []
            if level < level_count - 1:
                results.append(merge(level, table, pieces[i], their[i], before))
                continue
            if i:
                before.append(results[i - 1])
            shape = (trials, box_widths.shape[0], time_count)
            rows, out = detect(
                level, max(start, 0), shape, table, masks, pieces[i], their[i], before, out
            )
            results.append(rows)
        pieces = results
    if level_count == streamed:
        return out

    freq_rank = lax.axis_index("freq")
    dm_rows = jnp.concatenate(pieces, axis=1)[:, LANES:]
    for level_index in range(streamed, level_count):
        delay_reach = SHIFT_UNIT * 2**level_index
        tail_rows = shifted(dm_rows[:, time_count - delay_reach :], "tm", 1)
        own_rows = jnp.concatenate([tail_rows, dm_rows], axis=1)
        their_rows = swapped(own_rows, "freq", 2**level_index)
        is_upper = jnp.right_shift(freq_rank, level_index) % 2 == 1
        dm_rows = merge_level(own_rows, their_rows, merge_table[level_index], is_upper, delay_reach)
    tail_rows = shifted(dm_rows[:, time_count - (WMAX - 1) :], "tm", 1)
    return boxcar(jnp.concatenate([tail_rows, dm_rows], axis=1) / divisor, box_widths)


def solution(mesh):
    return jax.shard_map(
        body,
        mesh=mesh,
        in_specs=(P("freq", None, None, "tm"), P("freq", None), P(None, None, "freq"), P()),
        out_specs=P("freq", None, "tm"),
        check_vma=False,
    )
```

```python
import functools
import math

import jax
import jax.numpy as jnp
from jax import lax
from jax.experimental import pallas as pl
from jax.experimental.pallas import tpu as pltpu
from jax.sharding import PartitionSpec as P

TAPS = 4
LOCAL_MAX = 16
SHIFT_UNIT = 8
WMAX = 32
LANES = 128
OUT_COPIES = 2
UNIT = 2
SHARES = (19, 14)
PIECES = len(SHARES)
STREAMED = 3

epsilon = 1e-06

VM = pl.BlockSpec(memory_space=pltpu.VMEM)
SM = pl.BlockSpec(memory_space=pltpu.SMEM)
HBM = pl.BlockSpec(memory_space=pltpu.HBM)
PARAMS = pltpu.CompilerParams(vmem_limit_bytes=16 << 20)
SOURCE_LIMIT = 55_500_000
F32 = jnp.float32
BF16 = jnp.bfloat16


def swapped(value, axis, mask):
    pairs = [(source, source ^ mask) for source in range(lax.axis_size(axis))]
    return lax.ppermute(value, axis, pairs)


def shifted(block, axis, distance):
    devices = range(lax.axis_size(axis))
    route = [(i - distance, i) for i in devices if i - distance in devices]
    return lax.ppermute(block, axis, route)


def window_columns(branches):
    shape = (branches, LANES)
    place = (lane_index(shape) % TAPS * branches + row_index(shape)).astype(F32)
    length = TAPS * branches
    offset = (place - length / 2 + 0.5) * (math.pi / branches)
    hamming = 0.54 - 0.46 * jnp.cos(place * (2.0 * math.pi / (length - 1)))
    return jnp.sin(offset) / offset * hamming


def fourier_rows(branches):
    shape = (2 * branches, 4 * branches)
    row, column = row_index(shape), lane_index(shape)
    quarter = branches // 4
    turn = (row % branches) * (column % branches)
    turn = turn + jnp.where(row >= branches, 2 * quarter, quarter)
    turn = turn - jnp.where(column % (2 * branches) >= branches, quarter, 0)
    turn = turn % branches
    negative = turn > 2 * quarter
    turn = jnp.where(negative, turn - 2 * quarter, turn)
    turn = jnp.where(turn > quarter, 2 * quarter - turn, turn)
    value = jnp.zeros(shape, F32)
    for step in range(1, quarter + 1):
        value = jnp.where(turn == step, math.sin(2.0 * math.pi * step / branches), value)
    return jnp.where(negative, -value, value)


def halves(x):
    high = x.astype(BF16)
    return high, (x - high.astype(F32)).astype(BF16)


def thirds(x):
    high = x.astype(BF16)
    rest = x - high.astype(F32)
    middle = rest.astype(BF16)
    return high, middle, (rest - middle.astype(F32)).astype(BF16)


def lane_index(shape):
    return lax.broadcasted_iota(jnp.int32, shape, len(shape) - 1)


def row_index(shape):
    return lax.broadcasted_iota(jnp.int32, shape, 0)


def channel_kernel(
    pieces, x_hbm, power_ref, small_ref, big_ref, x_ref, win_ref, w_ref, sems
):
    rows, time_count = x_ref.shape
    branches = rows // 2
    width = time_count // pieces
    edge = TAPS - 1
    copies = []
    for piece in range(pieces):
        part = pl.ds(piece * width, width)
        copies.append(pltpu.make_async_copy(x_hbm.at[:, part], x_ref.at[:, part], sems.at[piece]))
        copies[-1].start()
    window = window_columns(branches)
    for tap in range(TAPS):
        column = jnp.broadcast_to(window[:, tap : tap + 1], (branches, LANES))
        win_ref[tap, :branches] = column
        win_ref[tap, branches:] = column
    w_ref[...] = jnp.concatenate(halves(fourier_rows(branches)), axis=1)

    group = 16
    lane = lane_index((group, LANES))
    nothing = jnp.zeros((group, LANES), F32)
    memory = [(nothing, nothing)] * (rows // group)
    total = jnp.zeros((branches, LANES), F32)
    tiles = time_count // LANES
    for tile in range(0, tiles + 1, UNIT):
        if tile < tiles and tile * LANES % width == 0:
            copies[tile * LANES // width].wait()
        unit = range(tile, min(tile + UNIT, tiles + 1))
        parts = {0: [], 1: []}
        for index in range(rows // group):
            part = slice(index * group, (index + 1) * group)
            older, sum_older = memory[index]
            row = {0: [], 1: []}
            for number in unit:
                if number < tiles:
                    here = x_ref[part, number * LANES : (number + 1) * LANES]
                    moved = pltpu.roll(here, 2, 1)
                    twice = jnp.where(lane < 2, older, moved)
                    even = win_ref[3, part] * here + win_ref[1, part] * twice
                    odd = win_ref[2, part] * here + win_ref[0, part] * twice
                else:
                    moved = nothing
                    twice = jnp.where(lane < 2, older, 0.0)
                    even = win_ref[1, part] * twice
                    odd = win_ref[0, part] * twice
                sum_moved = pltpu.roll(odd, 1, 1)
                filtered = even + jnp.where(lane < 1, sum_older, sum_moved)
                older, sum_older = moved, sum_moved
                for half, value in enumerate(halves(filtered)):
                    row[half].append(value)
            memory[index] = (older, sum_older)
            for half in range(2):
                parts[half].append(jnp.concatenate(row[half], axis=1))
        stack = jnp.concatenate(parts[0] + parts[1], axis=0)
        spectra = jnp.dot(
            w_ref[...], jnp.concatenate([stack, stack], axis=0), preferred_element_type=F32
        )
        for number in unit:
            value = spectra[:, (number - tile) * LANES : (number - tile + 1) * LANES]
            if number == 0:
                own = value
            if number == tiles:
                following = value
                continue
            power = value[:branches] ** 2 + value[branches:] ** 2
            power_ref[:, number * LANES : (number + 1) * LANES] = power
            if number == 0:
                power = jnp.where(lane_index(power.shape) >= edge, power, 0.0)
            total = total + power
    sums = jnp.sum(total, axis=1, keepdims=True)
    sums = jnp.concatenate([sums, jnp.zeros_like(sums)], axis=0)
    lane = lane_index((rows, LANES))
    packed = jnp.where(lane == 2 * edge, sums, 0.0)
    packed = jnp.where(lane < 2 * edge, pltpu.roll(own, edge, 1), packed)
    packed = jnp.where(lane < edge, following, packed)
    packed = jnp.concatenate([packed, jnp.zeros((LANES - rows, LANES), F32)], axis=0)
    packet = jnp.transpose(packed)[:8]
    small_ref[...] = packet
    big_ref[:8] = packet
    big_ref[8:] = power


def channelize(samples, pieces):
    rows, time_count = samples.shape
    branches = rows // 2
    return pl.pallas_call(
        functools.partial(channel_kernel, pieces),
        in_specs=[HBM],
        out_specs=[VM] * 3,
        out_shape=[
            jax.ShapeDtypeStruct((branches, time_count), F32),
            jax.ShapeDtypeStruct((8, LANES), F32),
            jax.ShapeDtypeStruct((8 + branches, LANES), F32),
        ],
        scratch_shapes=[
            pltpu.VMEM((rows, time_count), F32),
            pltpu.VMEM((TAPS, rows, LANES), F32),
            pltpu.VMEM((rows, 4 * rows), BF16),
            pltpu.SemaphoreType.DMA((pieces,)),
        ],
        compiler_params=pltpu.CompilerParams(vmem_limit_bytes=SOURCE_LIMIT),
        name="channelize",
    )(samples)


FINE = 2
PARTS = 3


def trial_rows(selector, trials, value, value_before, products_before):
    joined = jnp.concatenate([value_before, value], axis=1)
    stack = []
    for lag in range(FINE):
        moved = pltpu.roll(joined, lag, 1)[:, LANES:] if lag else value
        stack.extend(thirds(moved))
    products = jnp.dot(selector, jnp.concatenate(stack, axis=0), preferred_element_type=F32)
    rows = products[:trials]
    for step in range(1, LOCAL_MAX // FINE):
        part = slice(step * trials, (step + 1) * trials)
        both = jnp.concatenate([products_before[part], products[part]], axis=1)
        rows = rows + pltpu.roll(both, FINE * step, 1)[:, LANES:]
    width = value.shape[1]
    return rows, value[:, width - LANES :], products[:, width - LANES :]


def first_rows_kernel(peers, time_all, *refs):
    power_ref, packets, selector_ref = refs[0], refs[1 : 1 + peers], refs[1 + peers]
    rows_ref, scale_ref, line_ref, fold_ref = refs[2 + peers :]
    branches = power_ref.shape[0]
    trials = rows_ref.shape[0]
    rank = lax.axis_index("tm")
    edge = TAPS - 1

    line_ref[:8] = jnp.zeros((8, LANES), F32)
    for peer in range(peers):
        spot = pl.multiple_of(((rank ^ peer) + 1) * 8, 8)
        line_ref[pl.ds(spot, 8), :] = packets[peer][:8]
    mine = line_ref[8:]
    amplitude = mine + pltpu.roll(line_ref[: 8 * peers], edge, 0)
    square = amplitude * amplitude
    folded = square + pltpu.roll(square, LANES - branches, 1)
    fold_ref[...] = folded
    kind = row_index(mine.shape) % 8
    whole = jnp.where(kind == 2 * edge, mine, 0.0)
    whole = jnp.where((kind >= edge) & (kind < 2 * edge), folded, whole)
    band_mean = jnp.sum(whole, axis=0, keepdims=True) / time_all
    scale = 1.0 / (band_mean + epsilon)
    firsts = fold_ref[pl.ds(pl.multiple_of(rank * 8, 8), 8), :]
    firsts = jnp.where(row_index(firsts.shape) == 2 * edge, scale, firsts)
    columns = jnp.transpose(firsts)[:branches]
    scale = jnp.broadcast_to(columns[:, 2 * edge : 2 * edge + 1], (branches, LANES))
    scale_ref[...] = scale
    scale = scale[:, :1]

    tail = jnp.zeros((branches, LANES), F32)
    for peer in range(1, peers):
        if peer & (peer + 1) == 0:
            tail = jnp.where((rank ^ (rank - 1)) == peer, packets[peer][8:], tail)
    halo = jnp.where(rank > 0, tail * scale - 1.0, 0.0)
    start = power_ref[:, :LANES]
    for lane in range(edge):
        value = columns[:, edge + lane : edge + lane + 1]
        start = jnp.where(lane_index(start.shape) == lane, value, start)

    selector = selector_ref[...]
    width = rows_ref.shape[1] - LANES
    value = jnp.concatenate([start, power_ref[:, LANES:width]], axis=1) * scale - 1.0
    value = jnp.concatenate([halo, value], axis=1)
    nothing = jnp.zeros((selector.shape[0], LANES), F32)
    rows_ref[...], _, _ = trial_rows(selector, trials, value, jnp.zeros_like(halo), nothing)


def first_rows(power, packets, selector, tiles, time_all):
    branches = power.shape[0]
    trials = selector.shape[0] * FINE // LOCAL_MAX
    peers = len(packets)
    return pl.pallas_call(
        functools.partial(first_rows_kernel, peers, time_all),
        in_specs=[VM] * (2 + peers),
        out_specs=[VM] * 2,
        out_shape=[
            jax.ShapeDtypeStruct((trials, tiles * LANES), F32),
            jax.ShapeDtypeStruct((branches, LANES), F32),
        ],
        scratch_shapes=[
            pltpu.VMEM((8 * (peers + 1), LANES), F32),
            pltpu.VMEM((8 * peers, LANES), F32),
        ],
        compiler_params=PARAMS,
        name="first_rows",
    )(power, *packets, selector)


def more_rows_kernel(start, power_ref, scale_ref, selector_ref, rows_ref):
    trials, width = rows_ref.shape
    scale = scale_ref[:, :1]
    value = power_ref[:, start - LANES : start + width] * scale - 1.0
    selector = selector_ref[...]
    nothing = jnp.zeros((selector.shape[0], LANES), F32)
    rows, _, _ = trial_rows(selector, trials, value, jnp.zeros_like(value[:, :LANES]), nothing)
    rows_ref[...] = rows[:, LANES:]


def more_rows(power, scale, selector, start, tiles):
    trials = selector.shape[0] * FINE // LOCAL_MAX
    return pl.pallas_call(
        functools.partial(more_rows_kernel, start),
        in_specs=[VM] * 3,
        out_specs=VM,
        out_shape=jax.ShapeDtypeStruct((trials, tiles * LANES), F32),
        compiler_params=PARAMS,
        name="more_rows",
    )(power, scale, selector)


def delayed_rows(rows, amount):
    shape = (rows.shape[0], LANES)
    lane = lane_index(shape)
    amount = jnp.broadcast_to(amount, shape)
    source = (lane - amount) & (LANES - 1)
    tiles = [
        jnp.take_along_axis(rows[:, start : start + LANES], source, axis=1)
        for start in range(0, rows.shape[1], LANES)
    ]
    moved = [jnp.where(lane < amount, old, new) for old, new in zip(tiles, tiles[1:])]
    return jnp.concatenate(moved, axis=1)


def merged(level, first, refs):
    table_ref, own_ref, their_ref = refs[:3]
    trials, _ = own_ref.shape
    upper = (lax.axis_index("freq") >> level) & 1
    if first:
        before = jnp.zeros((trials, LANES), F32)
        own = jnp.concatenate([before, own_ref[...]], axis=1)
        their = jnp.concatenate([before, their_ref[...]], axis=1)
    else:
        own = jnp.concatenate([refs[3][:, refs[3].shape[1] - LANES :], own_ref[...]], axis=1)
        their = jnp.concatenate([refs[4][:, refs[4].shape[1] - LANES :], their_ref[...]], axis=1)
    table = table_ref[...].astype(jnp.int32)
    column = lane_index((trials, 2 * trials))
    low = table[:, 3 * level : 3 * level + 1] + upper * trials
    high = table[:, 3 * level + 1 : 3 * level + 2] + (1 - upper) * trials
    pick = jnp.concatenate([column == low, column == high], axis=0).astype(F32).astype(BF16)
    pick = jnp.concatenate([pick] * 3, axis=1)
    stack = jnp.concatenate(thirds(jnp.concatenate([own, their], axis=0)), axis=0)
    picked = jnp.dot(pick, stack, preferred_element_type=F32)
    delayed = picked[trials:]
    amount = table[:, 3 * level + 2 : 3 * level + 3]
    return picked[:trials, LANES:] + delayed_rows(delayed, amount)


def merge_kernel(level, first, *refs):
    refs[-1][...] = merged(level, first, refs[:-1])


def merge(level, table, own, their, before):
    return pl.pallas_call(
        functools.partial(merge_kernel, level, not before),
        in_specs=[VM] * (3 + len(before)),
        out_specs=VM,
        out_shape=jax.ShapeDtypeStruct(own.shape, F32),
        compiler_params=PARAMS,
        name="merge",
    )(table, own, their, *before)


def tables_kernel(divisor, width_ref, delay_ref, after_ref, selector_ref, mask_ref, factor_ref):
    del after_ref
    trials, channels = delay_ref.shape
    depth = FINE * PARTS * channels
    spread = row_index((channels, depth)) == lane_index((channels, depth)) % channels
    wanted = jnp.dot(
        delay_ref[...].astype(BF16), spread.astype(BF16), preferred_element_type=F32
    ).astype(jnp.int32)
    offset = lane_index((trials, depth)) // (PARTS * channels)
    coarse = LOCAL_MAX // FINE
    selector = jnp.concatenate(
        [(wanted == offset + FINE * step).astype(F32) for step in range(coarse)], axis=0
    ).astype(BF16)
    selector_ref[...] = selector

    shape = (2 * LANES, LANES)
    back = lane_index(shape) + LANES - row_index(shape)
    boxes = width_ref.shape[0]
    wide = jnp.ones(factor_ref.shape, jnp.int32)
    for box in range(boxes):
        inside = (back >= 0) & (back < width_ref[box])
        mask_ref[:, box * LANES : (box + 1) * LANES] = inside.astype(F32).astype(BF16)
        wide = jnp.where(row_index(wide.shape) == box, width_ref[box], wide)
    factor_ref[...] = 1.0 / (jnp.sqrt(wide.astype(F32)) * divisor)


def tables(widths, delays, divisor, after):
    boxes = widths.shape[0]
    trials, channels = delays.shape
    return pl.pallas_call(
        functools.partial(tables_kernel, divisor),
        in_specs=[SM, VM, VM],
        out_specs=[VM] * 3,
        out_shape=[
            jax.ShapeDtypeStruct((LOCAL_MAX // FINE * trials, FINE * PARTS * channels), BF16),
            jax.ShapeDtypeStruct((2 * LANES, boxes * LANES), BF16),
            jax.ShapeDtypeStruct((-(-boxes // 8) * 8, LANES), F32),
        ],
        compiler_params=PARAMS,
        name="tables",
    )(widths, delays, after)


def detect_kernel(level, start, keep, *refs):
    first = start == 0
    table_ref, mask_ref, factor_ref, own_ref, their_ref = refs[:5]
    out_ref, sem = refs[-2:]
    out_hbm = refs[-4] if keep else refs[-3]
    rows = merged(level, first, (table_ref, own_ref, their_ref, *refs[5:7]))
    if keep:
        refs[-3][...] = rows
    if not first:
        before = refs[7]
        rows = jnp.concatenate([before[:, before.shape[1] - LANES :], rows], axis=1)
    boxes, trials, width = out_ref.shape
    tiles = width // LANES
    mask = mask_ref[...]
    copies = []
    bounds = [tiles * part // OUT_COPIES for part in range(OUT_COPIES + 1)]
    for part, (begin, end) in enumerate(zip(bounds, bounds[1:])):
        pairs = [rows[:, tile * LANES : (tile + 2) * LANES] for tile in range(begin, end)]
        high, low = halves(jnp.concatenate(pairs, axis=0))
        sums = jnp.dot(high, mask, preferred_element_type=F32)
        sums = sums + jnp.dot(low, mask, preferred_element_type=F32)
        here = pl.ds(begin * LANES, (end - begin) * LANES)
        there = pl.ds(start + begin * LANES, (end - begin) * LANES)
        for box in range(boxes):
            factor = factor_ref[box : box + 1]
            for tile in range(begin, end):
                line = slice((tile - begin) * trials, (tile - begin + 1) * trials)
                value = sums[line, box * LANES : (box + 1) * LANES] * factor
                out_ref[box, :, tile * LANES : (tile + 1) * LANES] = value
            copies.append(
                pltpu.make_async_copy(
                    out_ref.at[box, :, here],
                    out_hbm.at[:, box, there],
                    sem.at[part, box],
                )
            )
            copies[-1].start()
    for copy in copies:
        copy.wait()


def detect(level, start, shape, table, masks, own, their, before, out):
    trials, width = own.shape
    operands = [table, *masks, own, their, *before]
    specs = [VM] * len(operands)
    aliases = {}
    if start == 0:
        width = width - LANES
    results = [jax.ShapeDtypeStruct(shape, F32)]
    if start + width < shape[2]:
        results.append(jax.ShapeDtypeStruct(own.shape, F32))
    if out is not None:
        aliases = {len(operands): 0}
        operands.append(out)
        specs.append(HBM)
    return pl.pallas_call(
        functools.partial(detect_kernel, level, start, len(results) > 1),
        in_specs=specs,
        out_specs=[HBM, VM][: len(results)],
        out_shape=results,
        scratch_shapes=[
            pltpu.VMEM((shape[1], trials, width), F32),
            pltpu.SemaphoreType.DMA((OUT_COPIES, shape[1])),
        ],
        input_output_aliases=aliases,
        compiler_params=PARAMS,
        name="detect",
    )(*operands)


def selector_rows(chosen, row_count):
    return (chosen[:, None] == jnp.arange(row_count, dtype=jnp.int32)[None, :]).astype(F32)


def delay_rows(picked_high, delay_amount, delay_reach):
    current = picked_high
    for bit_index in range(delay_reach.bit_length()):
        step_size = 2**bit_index
        moved = jnp.concatenate(
            [
                jnp.zeros((current.shape[0], step_size), F32),
                current[:, : current.shape[1] - step_size],
            ],
            axis=1,
        )
        bit_set = (jnp.right_shift(delay_amount, bit_index) % 2 == 1)[:, None]
        current = jnp.where(bit_set, moved, current)
    return current[:, delay_reach:]


def merge_level(own_rows, their_rows, level_table, is_upper, delay_reach):
    lower_rows = jnp.where(is_upper, their_rows, own_rows)
    upper_rows = jnp.where(is_upper, own_rows, their_rows)
    row_count = own_rows.shape[0]
    pick = functools.partial(jnp.dot, precision=lax.Precision.HIGHEST, preferred_element_type=F32)
    picked_low = pick(selector_rows(level_table[0], row_count), lower_rows[:, delay_reach:])
    picked_high = pick(selector_rows(level_table[1], row_count), upper_rows)
    return picked_low + delay_rows(picked_high, level_table[2], delay_reach)


def boxcar(dedispersed, widths):
    time_count = dedispersed.shape[1] - (WMAX - 1)
    detection = jnp.zeros((dedispersed.shape[0], widths.shape[0], time_count), F32)
    for offset in range(WMAX):
        width_mask = (offset < widths).astype(F32)
        lagged = dedispersed[:, WMAX - 1 - offset : WMAX - 1 - offset + time_count]
        detection = detection + lagged[:, None, :] * width_mask[None, :, None]
    return detection / jnp.sqrt(widths.astype(F32))[None, :, None]


def body(voltages, local_delay, merge_table, box_widths):
    branches = voltages.shape[2]
    time_count = voltages.shape[3]
    freq_size = lax.axis_size("freq")
    tm_size = lax.axis_size("tm")
    level_count = freq_size.bit_length() - 1
    streamed = min(STREAMED, level_count)
    trials = local_delay.shape[0]
    divisor = math.sqrt(branches * freq_size)

    power, small, big = channelize(voltages.reshape(2 * branches, time_count), 4)
    packets = [small]
    for peer in range(1, tm_size):
        packets.append(swapped(big if peer & (peer + 1) == 0 else small, "tm", peer))

    table = merge_table[:streamed].reshape(3 * streamed, trials).T.astype(F32)
    table = jnp.pad(table, ((0, 0), (0, LANES - 3 * streamed)))
    tiles = 1 + time_count // LANES
    sizes = [tiles * share // sum(SHARES) for share in SHARES]
    sizes[-1] += tiles - sum(sizes)
    starts = [sum(sizes[:i]) * LANES - LANES for i in range(len(sizes))]
    selector, *masks = tables(box_widths, local_delay, divisor, small)
    rows, scale = first_rows(power, packets, selector, sizes[0], float(time_count * tm_size))
    pieces = [rows]
    for i in range(1, PIECES):
        pieces.append(more_rows(power, scale, selector, starts[i], sizes[i]))

    for level in range(streamed):
        their = []
        for piece in pieces:
            their.append(swapped(piece, "freq", 2**level))
        results = []
        out = None
        for i, start in enumerate(starts):
            before = [pieces[i - 1], their[i - 1]] if i else []
            if level < level_count - 1:
                results.append(merge(level, table, pieces[i], their[i], before))
                continue
            if i:
                before.append(results[i - 1])
            shape = (trials, box_widths.shape[0], time_count)
            out, *rows = detect(
                level, max(start, 0), shape, table, masks, pieces[i], their[i], before, out
            )
            results.extend(rows)
        pieces = results
    if level_count == streamed:
        return out

    freq_rank = lax.axis_index("freq")
    dm_rows = jnp.concatenate(pieces, axis=1)[:, LANES:]
    for level_index in range(streamed, level_count):
        delay_reach = SHIFT_UNIT * 2**level_index
        tail_rows = shifted(dm_rows[:, time_count - delay_reach :], "tm", 1)
        own_rows = jnp.concatenate([tail_rows, dm_rows], axis=1)
        their_rows = swapped(own_rows, "freq", 2**level_index)
        is_upper = jnp.right_shift(freq_rank, level_index) % 2 == 1
        dm_rows = merge_level(own_rows, their_rows, merge_table[level_index], is_upper, delay_reach)
    tail_rows = shifted(dm_rows[:, time_count - (WMAX - 1) :], "tm", 1)
    return boxcar(jnp.concatenate([tail_rows, dm_rows], axis=1) / divisor, box_widths)


def solution(mesh):
    return jax.shard_map(
        body,
        mesh=mesh,
        in_specs=(P("freq", None, None, "tm"), P("freq", None), P(None, None, "freq"), P()),
        out_specs=P("freq", None, "tm"),
        check_vma=False,
    )
```

```python
import functools
import math

import jax
import jax.numpy as jnp
from jax import lax
from jax.experimental import pallas as pl
from jax.experimental.pallas import tpu as pltpu
from jax.sharding import PartitionSpec as P

TAPS = 4
LOCAL_MAX = 16
SHIFT_UNIT = 8
WMAX = 32
LANES = 128
OUT_COPIES = 2
FETCHES = 2
UNIT = 2
SHARES = (19, 14)
PIECES = len(SHARES)
STREAMED = 3

epsilon = 1e-06

VM = pl.BlockSpec(memory_space=pltpu.VMEM)
SM = pl.BlockSpec(memory_space=pltpu.SMEM)
HBM = pl.BlockSpec(memory_space=pltpu.HBM)
PARAMS = pltpu.CompilerParams(vmem_limit_bytes=16 << 20)
SOURCE_LIMIT = 55_500_000
F32 = jnp.float32
BF16 = jnp.bfloat16


def swapped(value, axis, mask):
    pairs = [(source, source ^ mask) for source in range(lax.axis_size(axis))]
    return lax.ppermute(value, axis, pairs)


def shifted(block, axis, distance):
    devices = range(lax.axis_size(axis))
    route = [(i - distance, i) for i in devices if i - distance in devices]
    return lax.ppermute(block, axis, route)


def window_columns(branches):
    shape = (branches, LANES)
    place = (lane_index(shape) % TAPS * branches + row_index(shape)).astype(F32)
    length = TAPS * branches
    offset = (place - length / 2 + 0.5) * (math.pi / branches)
    hamming = 0.54 - 0.46 * jnp.cos(place * (2.0 * math.pi / (length - 1)))
    return jnp.sin(offset) / offset * hamming


def fourier_rows(branches):
    shape = (2 * branches, 4 * branches)
    row, column = row_index(shape), lane_index(shape)
    quarter = branches // 4
    turn = (row % branches) * (column % branches)
    turn = turn + jnp.where(row >= branches, 2 * quarter, quarter)
    turn = turn - jnp.where(column % (2 * branches) >= branches, quarter, 0)
    turn = turn % branches
    negative = turn > 2 * quarter
    turn = jnp.where(negative, turn - 2 * quarter, turn)
    turn = jnp.where(turn > quarter, 2 * quarter - turn, turn)
    value = jnp.zeros(shape, F32)
    for step in range(1, quarter + 1):
        value = jnp.where(turn == step, math.sin(2.0 * math.pi * step / branches), value)
    return jnp.where(negative, -value, value)


def halves(x):
    high = x.astype(BF16)
    return high, (x - high.astype(F32)).astype(BF16)


def thirds(x):
    high = x.astype(BF16)
    rest = x - high.astype(F32)
    middle = rest.astype(BF16)
    return high, middle, (rest - middle.astype(F32)).astype(BF16)


def lane_index(shape):
    return lax.broadcasted_iota(jnp.int32, shape, len(shape) - 1)


def row_index(shape):
    return lax.broadcasted_iota(jnp.int32, shape, 0)


def channel_kernel(
    pieces, x_hbm, power_ref, small_ref, big_ref, x_ref, win_ref, w_ref, sems
):
    rows, time_count = x_ref.shape
    branches = rows // 2
    width = time_count // pieces
    edge = TAPS - 1
    copies = []
    for piece in range(pieces):
        part = pl.ds(piece * width, width)
        copies.append(pltpu.make_async_copy(x_hbm.at[:, part], x_ref.at[:, part], sems.at[piece]))
        copies[-1].start()
    window = window_columns(branches)
    for tap in range(TAPS):
        column = jnp.broadcast_to(window[:, tap : tap + 1], (branches, LANES))
        win_ref[tap, :branches] = column
        win_ref[tap, branches:] = column
    w_ref[...] = jnp.concatenate(halves(fourier_rows(branches)), axis=1)

    group = 16
    lane = lane_index((group, LANES))
    nothing = jnp.zeros((group, LANES), F32)
    memory = [(nothing, nothing)] * (rows // group)
    total = jnp.zeros((branches, LANES), F32)
    tiles = time_count // LANES
    for tile in range(0, tiles + 1, UNIT):
        if tile < tiles and tile * LANES % width == 0:
            copies[tile * LANES // width].wait()
        unit = range(tile, min(tile + UNIT, tiles + 1))
        parts = {0: [], 1: []}
        for index in range(rows // group):
            part = slice(index * group, (index + 1) * group)
            older, sum_older = memory[index]
            row = {0: [], 1: []}
            for number in unit:
                if number < tiles:
                    here = x_ref[part, number * LANES : (number + 1) * LANES]
                    moved = pltpu.roll(here, 2, 1)
                    twice = jnp.where(lane < 2, older, moved)
                    even = win_ref[3, part] * here + win_ref[1, part] * twice
                    odd = win_ref[2, part] * here + win_ref[0, part] * twice
                else:
                    moved = nothing
                    twice = jnp.where(lane < 2, older, 0.0)
                    even = win_ref[1, part] * twice
                    odd = win_ref[0, part] * twice
                sum_moved = pltpu.roll(odd, 1, 1)
                filtered = even + jnp.where(lane < 1, sum_older, sum_moved)
                older, sum_older = moved, sum_moved
                for half, value in enumerate(halves(filtered)):
                    row[half].append(value)
            memory[index] = (older, sum_older)
            for half in range(2):
                parts[half].append(jnp.concatenate(row[half], axis=1))
        stack = jnp.concatenate(parts[0] + parts[1], axis=0)
        spectra = jnp.dot(
            w_ref[...], jnp.concatenate([stack, stack], axis=0), preferred_element_type=F32
        )
        for number in unit:
            value = spectra[:, (number - tile) * LANES : (number - tile + 1) * LANES]
            if number == 0:
                own = value
            if number == tiles:
                following = value
                continue
            power = value[:branches] ** 2 + value[branches:] ** 2
            power_ref[:, number * LANES : (number + 1) * LANES] = power
            if number == 0:
                power = jnp.where(lane_index(power.shape) >= edge, power, 0.0)
            total = total + power
    sums = jnp.sum(total, axis=1, keepdims=True)
    sums = jnp.concatenate([sums, jnp.zeros_like(sums)], axis=0)
    lane = lane_index((rows, LANES))
    packed = jnp.where(lane == 2 * edge, sums, 0.0)
    packed = jnp.where(lane < 2 * edge, pltpu.roll(own, edge, 1), packed)
    packed = jnp.where(lane < edge, following, packed)
    packed = jnp.concatenate([packed, jnp.zeros((LANES - rows, LANES), F32)], axis=0)
    packet = jnp.transpose(packed)[:8]
    small_ref[...] = packet
    big_ref[:8] = packet
    big_ref[8:] = power


def channelize(samples, pieces):
    rows, time_count = samples.shape
    branches = rows // 2
    return pl.pallas_call(
        functools.partial(channel_kernel, pieces),
        in_specs=[HBM],
        out_specs=[VM] * 3,
        out_shape=[
            jax.ShapeDtypeStruct((branches, time_count), F32),
            jax.ShapeDtypeStruct((8, LANES), F32),
            jax.ShapeDtypeStruct((8 + branches, LANES), F32),
        ],
        scratch_shapes=[
            pltpu.VMEM((rows, time_count), F32),
            pltpu.VMEM((TAPS, rows, LANES), F32),
            pltpu.VMEM((rows, 4 * rows), BF16),
            pltpu.SemaphoreType.DMA((pieces,)),
        ],
        compiler_params=pltpu.CompilerParams(vmem_limit_bytes=SOURCE_LIMIT),
        name="channelize",
    )(samples)


FINE = 2
PARTS = 3


def trial_rows(selector, trials, value, value_before, products_before):
    joined = jnp.concatenate([value_before, value], axis=1)
    stack = []
    for lag in range(FINE):
        moved = pltpu.roll(joined, lag, 1)[:, LANES:] if lag else value
        stack.extend(thirds(moved))
    products = jnp.dot(selector, jnp.concatenate(stack, axis=0), preferred_element_type=F32)
    rows = products[:trials]
    for step in range(1, LOCAL_MAX // FINE):
        part = slice(step * trials, (step + 1) * trials)
        both = jnp.concatenate([products_before[part], products[part]], axis=1)
        rows = rows + pltpu.roll(both, FINE * step, 1)[:, LANES:]
    width = value.shape[1]
    return rows, value[:, width - LANES :], products[:, width - LANES :]


def first_rows_kernel(peers, time_all, *refs):
    power_ref, packets, selector_ref = refs[0], refs[1 : 1 + peers], refs[1 + peers]
    rows_ref, scale_ref, line_ref, fold_ref = refs[2 + peers :]
    branches = power_ref.shape[0]
    trials = rows_ref.shape[0]
    rank = lax.axis_index("tm")
    edge = TAPS - 1

    line_ref[:8] = jnp.zeros((8, LANES), F32)
    for peer in range(peers):
        spot = pl.multiple_of(((rank ^ peer) + 1) * 8, 8)
        line_ref[pl.ds(spot, 8), :] = packets[peer][:8]
    mine = line_ref[8:]
    amplitude = mine + pltpu.roll(line_ref[: 8 * peers], edge, 0)
    square = amplitude * amplitude
    folded = square + pltpu.roll(square, LANES - branches, 1)
    fold_ref[...] = folded
    kind = row_index(mine.shape) % 8
    whole = jnp.where(kind == 2 * edge, mine, 0.0)
    whole = jnp.where((kind >= edge) & (kind < 2 * edge), folded, whole)
    band_mean = jnp.sum(whole, axis=0, keepdims=True) / time_all
    scale = 1.0 / (band_mean + epsilon)
    firsts = fold_ref[pl.ds(pl.multiple_of(rank * 8, 8), 8), :]
    firsts = jnp.where(row_index(firsts.shape) == 2 * edge, scale, firsts)
    columns = jnp.transpose(firsts)[:branches]
    scale = jnp.broadcast_to(columns[:, 2 * edge : 2 * edge + 1], (branches, LANES))
    scale_ref[...] = scale
    scale = scale[:, :1]

    tail = jnp.zeros((branches, LANES), F32)
    for peer in range(1, peers):
        if peer & (peer + 1) == 0:
            tail = jnp.where((rank ^ (rank - 1)) == peer, packets[peer][8:], tail)
    halo = jnp.where(rank > 0, tail * scale - 1.0, 0.0)
    start = power_ref[:, :LANES]
    for lane in range(edge):
        value = columns[:, edge + lane : edge + lane + 1]
        start = jnp.where(lane_index(start.shape) == lane, value, start)

    selector = selector_ref[...]
    width = rows_ref.shape[1] - LANES
    value = jnp.concatenate([start, power_ref[:, LANES:width]], axis=1) * scale - 1.0
    value = jnp.concatenate([halo, value], axis=1)
    nothing = jnp.zeros((selector.shape[0], LANES), F32)
    rows_ref[...], _, _ = trial_rows(selector, trials, value, jnp.zeros_like(halo), nothing)


def first_rows(power, packets, selector, tiles, time_all):
    branches = power.shape[0]
    trials = selector.shape[0] * FINE // LOCAL_MAX
    peers = len(packets)
    return pl.pallas_call(
        functools.partial(first_rows_kernel, peers, time_all),
        in_specs=[VM] * (2 + peers),
        out_specs=[VM] * 2,
        out_shape=[
            jax.ShapeDtypeStruct((trials, tiles * LANES), F32),
            jax.ShapeDtypeStruct((branches, LANES), F32),
        ],
        scratch_shapes=[
            pltpu.VMEM((8 * (peers + 1), LANES), F32),
            pltpu.VMEM((8 * peers, LANES), F32),
        ],
        compiler_params=PARAMS,
        name="first_rows",
    )(power, *packets, selector)


def more_rows_kernel(start, power_ref, scale_ref, selector_ref, rows_ref):
    trials, width = rows_ref.shape
    scale = scale_ref[:, :1]
    value = power_ref[:, start - LANES : start + width] * scale - 1.0
    selector = selector_ref[...]
    nothing = jnp.zeros((selector.shape[0], LANES), F32)
    rows, _, _ = trial_rows(selector, trials, value, jnp.zeros_like(value[:, :LANES]), nothing)
    rows_ref[...] = rows[:, LANES:]


def more_rows(power, scale, selector, start, tiles):
    trials = selector.shape[0] * FINE // LOCAL_MAX
    return pl.pallas_call(
        functools.partial(more_rows_kernel, start),
        in_specs=[VM] * 3,
        out_specs=VM,
        out_shape=jax.ShapeDtypeStruct((trials, tiles * LANES), F32),
        compiler_params=PARAMS,
        name="more_rows",
    )(power, scale, selector)


def delayed_rows(rows, amount):
    shape = (rows.shape[0], LANES)
    lane = lane_index(shape)
    amount = jnp.broadcast_to(amount, shape)
    source = (lane - amount) & (LANES - 1)
    tiles = [
        jnp.take_along_axis(rows[:, start : start + LANES], source, axis=1)
        for start in range(0, rows.shape[1], LANES)
    ]
    moved = [jnp.where(lane < amount, old, new) for old, new in zip(tiles, tiles[1:])]
    return jnp.concatenate(moved, axis=1)


def merged(level, first, refs):
    table_ref, own_ref, their_ref = refs[:3]
    trials, _ = own_ref.shape
    upper = (lax.axis_index("freq") >> level) & 1
    if first:
        before = jnp.zeros((trials, LANES), F32)
        own = jnp.concatenate([before, own_ref[...]], axis=1)
        their = jnp.concatenate([before, their_ref[...]], axis=1)
    else:
        own = jnp.concatenate([refs[3][:, refs[3].shape[1] - LANES :], own_ref[...]], axis=1)
        their = jnp.concatenate([refs[4][:, refs[4].shape[1] - LANES :], their_ref[...]], axis=1)
    table = table_ref[...].astype(jnp.int32)
    column = lane_index((trials, 2 * trials))
    low = table[:, 3 * level : 3 * level + 1] + upper * trials
    high = table[:, 3 * level + 1 : 3 * level + 2] + (1 - upper) * trials
    pick = jnp.concatenate([column == low, column == high], axis=0).astype(F32).astype(BF16)
    pick = jnp.concatenate([pick] * 3, axis=1)
    stack = jnp.concatenate(thirds(jnp.concatenate([own, their], axis=0)), axis=0)
    picked = jnp.dot(pick, stack, preferred_element_type=F32)
    delayed = picked[trials:]
    amount = table[:, 3 * level + 2 : 3 * level + 3]
    return picked[:trials, LANES:] + delayed_rows(delayed, amount)


def merge_kernel(level, first, *refs):
    refs[-1][...] = merged(level, first, refs[:-1])


def merge(level, table, own, their, before):
    return pl.pallas_call(
        functools.partial(merge_kernel, level, not before),
        in_specs=[VM] * (3 + len(before)),
        out_specs=VM,
        out_shape=jax.ShapeDtypeStruct(own.shape, F32),
        compiler_params=PARAMS,
        name="merge",
    )(table, own, their, *before)


def tables_kernel(divisor, width_ref, delay_ref, after_ref, selector_ref, mask_ref, factor_ref):
    del after_ref
    trials, channels = delay_ref.shape
    depth = FINE * PARTS * channels
    spread = row_index((channels, depth)) == lane_index((channels, depth)) % channels
    wanted = jnp.dot(
        delay_ref[...].astype(BF16), spread.astype(BF16), preferred_element_type=F32
    ).astype(jnp.int32)
    offset = lane_index((trials, depth)) // (PARTS * channels)
    coarse = LOCAL_MAX // FINE
    selector = jnp.concatenate(
        [(wanted == offset + FINE * step).astype(F32) for step in range(coarse)], axis=0
    ).astype(BF16)
    selector_ref[...] = selector

    shape = (2 * LANES, LANES)
    back = lane_index(shape) + LANES - row_index(shape)
    boxes = width_ref.shape[0]
    wide = jnp.ones(factor_ref.shape, jnp.int32)
    for box in range(boxes):
        inside = (back >= 0) & (back < width_ref[box])
        mask_ref[:, box * LANES : (box + 1) * LANES] = inside.astype(F32).astype(BF16)
        wide = jnp.where(row_index(wide.shape) == box, width_ref[box], wide)
    factor_ref[...] = 1.0 / (jnp.sqrt(wide.astype(F32)) * divisor)


def tables(widths, delays, divisor, after):
    boxes = widths.shape[0]
    trials, channels = delays.shape
    return pl.pallas_call(
        functools.partial(tables_kernel, divisor),
        in_specs=[SM, VM, VM],
        out_specs=[VM] * 3,
        out_shape=[
            jax.ShapeDtypeStruct((LOCAL_MAX // FINE * trials, FINE * PARTS * channels), BF16),
            jax.ShapeDtypeStruct((2 * LANES, boxes * LANES), BF16),
            jax.ShapeDtypeStruct((-(-boxes // 8) * 8, LANES), F32),
        ],
        compiler_params=PARAMS,
        name="tables",
    )(widths, delays, after)


def boxcar_pieces(rows, mask_ref, factor_ref, out_ref, begin, end):
    boxes, trials, _ = out_ref.shape
    pairs = [rows[:, tile * LANES : (tile + 2) * LANES] for tile in range(begin, end)]
    high, low = halves(jnp.concatenate(pairs, axis=0))
    mask = mask_ref[...]
    sums = jnp.dot(high, mask, preferred_element_type=F32)
    sums = sums + jnp.dot(low, mask, preferred_element_type=F32)
    for box in range(boxes):
        factor = factor_ref[box : box + 1]
        for tile in range(begin, end):
            line = slice((tile - begin) * trials, (tile - begin + 1) * trials)
            value = sums[line, box * LANES : (box + 1) * LANES] * factor
            out_ref[box, :, tile * LANES : (tile + 1) * LANES] = value


def detect_kernel(level, first, *refs):
    table_ref, mask_ref, factor_ref, own_ref, their_ref = refs[:5]
    rows_ref, out_ref = refs[-2:]
    rows = merged(level, first, (table_ref, own_ref, their_ref, *refs[5:7]))
    rows_ref[...] = rows
    if not first:
        before = refs[7]
        rows = jnp.concatenate([before[:, before.shape[1] - LANES :], rows], axis=1)
    boxcar_pieces(rows, mask_ref, factor_ref, out_ref, 0, out_ref.shape[2] // LANES)


def detect(level, table, masks, own, their, before):
    trials, width = own.shape
    operands = [table, *masks, own, their, *before]
    boxes = masks[0].shape[1] // LANES
    if not before:
        width = width - LANES
    return pl.pallas_call(
        functools.partial(detect_kernel, level, not before),
        in_specs=[VM] * len(operands),
        out_specs=[VM] * 2,
        out_shape=[
            jax.ShapeDtypeStruct(own.shape, F32),
            jax.ShapeDtypeStruct((boxes, trials, width), F32),
        ],
        compiler_params=PARAMS,
        name="detect",
    )(*operands)


def finish_kernel(level, *refs):
    table_ref, mask_ref, factor_ref, own_ref, their_ref = refs[:5]
    before, ready = refs[7], refs[8:-3]
    out_hbm, out_ref, sem = refs[-3:]
    boxes = out_ref.shape[0]
    copies = []

    def write(source, box, begin, end, start):
        number = len(copies)
        copies.append(
            pltpu.make_async_copy(
                source.at[box, :, pl.ds(begin, end - begin)],
                out_hbm.at[:, box, pl.ds(start + begin, end - begin)],
                sem.at[number],
            )
        )
        copies[-1].start()

    start = 0
    for piece in ready:
        for box in range(boxes):
            write(piece, box, 0, piece.shape[2], start)
        start += piece.shape[2]
    rows = merged(level, False, (table_ref, own_ref, their_ref, *refs[5:7]))
    rows = jnp.concatenate([before[:, before.shape[1] - LANES :], rows], axis=1)
    tiles = out_ref.shape[2] // LANES
    bounds = [tiles * part // OUT_COPIES for part in range(OUT_COPIES + 1)]
    for begin, end in zip(bounds, bounds[1:]):
        boxcar_pieces(rows, mask_ref, factor_ref, out_ref, begin, end)
        for box in range(boxes):
            write(out_ref, box, begin * LANES, end * LANES, start)
    for copy in copies:
        copy.wait()


def finish(level, table, masks, own, their, before, ready):
    trials, width = own.shape
    operands = [table, *masks, own, their, *before, *ready]
    boxes = masks[0].shape[1] // LANES
    time_count = width + sum(piece.shape[2] for piece in ready)
    return pl.pallas_call(
        functools.partial(finish_kernel, level),
        in_specs=[VM] * len(operands),
        out_specs=HBM,
        out_shape=jax.ShapeDtypeStruct((trials, boxes, time_count), F32),
        scratch_shapes=[
            pltpu.VMEM((boxes, trials, width), F32),
            pltpu.SemaphoreType.DMA((boxes * (len(ready) + OUT_COPIES),)),
        ],
        compiler_params=PARAMS,
        name="finish",
    )(*operands)


def selector_rows(chosen, row_count):
    return (chosen[:, None] == jnp.arange(row_count, dtype=jnp.int32)[None, :]).astype(F32)


def delay_rows(picked_high, delay_amount, delay_reach):
    current = picked_high
    for bit_index in range(delay_reach.bit_length()):
        step_size = 2**bit_index
        moved = jnp.concatenate(
            [
                jnp.zeros((current.shape[0], step_size), F32),
                current[:, : current.shape[1] - step_size],
            ],
            axis=1,
        )
        bit_set = (jnp.right_shift(delay_amount, bit_index) % 2 == 1)[:, None]
        current = jnp.where(bit_set, moved, current)
    return current[:, delay_reach:]


def merge_level(own_rows, their_rows, level_table, is_upper, delay_reach):
    lower_rows = jnp.where(is_upper, their_rows, own_rows)
    upper_rows = jnp.where(is_upper, own_rows, their_rows)
    row_count = own_rows.shape[0]
    pick = functools.partial(jnp.dot, precision=lax.Precision.HIGHEST, preferred_element_type=F32)
    picked_low = pick(selector_rows(level_table[0], row_count), lower_rows[:, delay_reach:])
    picked_high = pick(selector_rows(level_table[1], row_count), upper_rows)
    return picked_low + delay_rows(picked_high, level_table[2], delay_reach)


def boxcar(dedispersed, widths):
    time_count = dedispersed.shape[1] - (WMAX - 1)
    detection = jnp.zeros((dedispersed.shape[0], widths.shape[0], time_count), F32)
    for offset in range(WMAX):
        width_mask = (offset < widths).astype(F32)
        lagged = dedispersed[:, WMAX - 1 - offset : WMAX - 1 - offset + time_count]
        detection = detection + lagged[:, None, :] * width_mask[None, :, None]
    return detection / jnp.sqrt(widths.astype(F32))[None, :, None]


def body(voltages, local_delay, merge_table, box_widths):
    branches = voltages.shape[2]
    time_count = voltages.shape[3]
    freq_size = lax.axis_size("freq")
    tm_size = lax.axis_size("tm")
    level_count = freq_size.bit_length() - 1
    streamed = min(STREAMED, level_count)
    trials = local_delay.shape[0]
    divisor = math.sqrt(branches * freq_size)

    power, small, big = channelize(voltages.reshape(2 * branches, time_count), FETCHES)
    packets = [small]
    for peer in range(1, tm_size):
        packets.append(swapped(big if peer & (peer + 1) == 0 else small, "tm", peer))

    table = merge_table[:streamed].reshape(3 * streamed, trials).T.astype(F32)
    table = jnp.pad(table, ((0, 0), (0, LANES - 3 * streamed)))
    tiles = 1 + time_count // LANES
    sizes = [tiles * share // sum(SHARES) for share in SHARES]
    sizes[-1] += tiles - sum(sizes)
    starts = [sum(sizes[:i]) * LANES - LANES for i in range(len(sizes))]
    selector, *masks = tables(box_widths, local_delay, divisor, small)
    rows, scale = first_rows(power, packets, selector, sizes[0], float(time_count * tm_size))
    pieces = [rows]
    for i in range(1, PIECES):
        pieces.append(more_rows(power, scale, selector, starts[i], sizes[i]))

    for level in range(streamed):
        their = []
        for piece in pieces:
            their.append(swapped(piece, "freq", 2**level))
        results = []
        ready = []
        for i in range(PIECES):
            before = [pieces[i - 1], their[i - 1]] if i else []
            if level < level_count - 1:
                results.append(merge(level, table, pieces[i], their[i], before))
                continue
            if i:
                before.append(results[i - 1])
            if i == PIECES - 1:
                return finish(level, table, masks, pieces[i], their[i], before, ready)
            rows, boxed = detect(level, table, masks, pieces[i], their[i], before)
            results.append(rows)
            ready.append(boxed)
        pieces = results
    freq_rank = lax.axis_index("freq")
    dm_rows = jnp.concatenate(pieces, axis=1)[:, LANES:]
    for level_index in range(streamed, level_count):
        delay_reach = SHIFT_UNIT * 2**level_index
        tail_rows = shifted(dm_rows[:, time_count - delay_reach :], "tm", 1)
        own_rows = jnp.concatenate([tail_rows, dm_rows], axis=1)
        their_rows = swapped(own_rows, "freq", 2**level_index)
        is_upper = jnp.right_shift(freq_rank, level_index) % 2 == 1
        dm_rows = merge_level(own_rows, their_rows, merge_table[level_index], is_upper, delay_reach)
    tail_rows = shifted(dm_rows[:, time_count - (WMAX - 1) :], "tm", 1)
    return boxcar(jnp.concatenate([tail_rows, dm_rows], axis=1) / divisor, box_widths)


def solution(mesh):
    return jax.shard_map(
        body,
        mesh=mesh,
        in_specs=(P("freq", None, None, "tm"), P("freq", None), P(None, None, "freq"), P()),
        out_specs=P("freq", None, "tm"),
        check_vma=False,
    )
```

```python
import functools
import math

import jax
import jax.numpy as jnp
from jax import lax
from jax.experimental import pallas as pl
from jax.experimental.pallas import tpu as pltpu
from jax.sharding import PartitionSpec as P

TAPS = 4
LOCAL_MAX = 16
SHIFT_UNIT = 8
WMAX = 32
LANES = 128
OUT_COPIES = 2
FETCHES = 2
UNIT = 2
SHARES = (19, 8, 6)
PIECES = len(SHARES)
STREAMED = 3

epsilon = 1e-06

VM = pl.BlockSpec(memory_space=pltpu.VMEM)
SM = pl.BlockSpec(memory_space=pltpu.SMEM)
HBM = pl.BlockSpec(memory_space=pltpu.HBM)
PARAMS = pltpu.CompilerParams(vmem_limit_bytes=16 << 20)
SOURCE_LIMIT = 55_500_000
F32 = jnp.float32
BF16 = jnp.bfloat16


def swapped(value, axis, mask):
    pairs = [(source, source ^ mask) for source in range(lax.axis_size(axis))]
    return lax.ppermute(value, axis, pairs)


def shifted(block, axis, distance):
    devices = range(lax.axis_size(axis))
    route = [(i - distance, i) for i in devices if i - distance in devices]
    return lax.ppermute(block, axis, route)


def window_columns(branches):
    shape = (branches, LANES)
    place = (lane_index(shape) % TAPS * branches + row_index(shape)).astype(F32)
    length = TAPS * branches
    offset = (place - length / 2 + 0.5) * (math.pi / branches)
    hamming = 0.54 - 0.46 * jnp.cos(place * (2.0 * math.pi / (length - 1)))
    return jnp.sin(offset) / offset * hamming


def fourier_rows(branches):
    shape = (2 * branches, 4 * branches)
    row, column = row_index(shape), lane_index(shape)
    quarter = branches // 4
    turn = (row % branches) * (column % branches)
    turn = turn + jnp.where(row >= branches, 2 * quarter, quarter)
    turn = turn - jnp.where(column % (2 * branches) >= branches, quarter, 0)
    turn = turn % branches
    negative = turn > 2 * quarter
    turn = jnp.where(negative, turn - 2 * quarter, turn)
    turn = jnp.where(turn > quarter, 2 * quarter - turn, turn)
    value = jnp.zeros(shape, F32)
    for step in range(1, quarter + 1):
        value = jnp.where(turn == step, math.sin(2.0 * math.pi * step / branches), value)
    return jnp.where(negative, -value, value)


def halves(x):
    high = x.astype(BF16)
    return high, (x - high.astype(F32)).astype(BF16)


def thirds(x):
    high = x.astype(BF16)
    rest = x - high.astype(F32)
    middle = rest.astype(BF16)
    return high, middle, (rest - middle.astype(F32)).astype(BF16)


def lane_index(shape):
    return lax.broadcasted_iota(jnp.int32, shape, len(shape) - 1)


def row_index(shape):
    return lax.broadcasted_iota(jnp.int32, shape, 0)


def channel_kernel(
    pieces, x_hbm, power_ref, small_ref, big_ref, x_ref, win_ref, w_ref, sems
):
    rows, time_count = x_ref.shape
    branches = rows // 2
    width = time_count // pieces
    edge = TAPS - 1
    copies = []
    for piece in range(pieces):
        part = pl.ds(piece * width, width)
        copies.append(pltpu.make_async_copy(x_hbm.at[:, part], x_ref.at[:, part], sems.at[piece]))
        copies[-1].start()
    window = window_columns(branches)
    for tap in range(TAPS):
        column = jnp.broadcast_to(window[:, tap : tap + 1], (branches, LANES))
        win_ref[tap, :branches] = column
        win_ref[tap, branches:] = column
    w_ref[...] = jnp.concatenate(halves(fourier_rows(branches)), axis=1)

    group = 16
    lane = lane_index((group, LANES))
    nothing = jnp.zeros((group, LANES), F32)
    memory = [(nothing, nothing)] * (rows // group)
    total = jnp.zeros((branches, LANES), F32)
    tiles = time_count // LANES
    for tile in range(0, tiles + 1, UNIT):
        if tile < tiles and tile * LANES % width == 0:
            copies[tile * LANES // width].wait()
        unit = range(tile, min(tile + UNIT, tiles + 1))
        parts = {0: [], 1: []}
        for index in range(rows // group):
            part = slice(index * group, (index + 1) * group)
            older, sum_older = memory[index]
            row = {0: [], 1: []}
            for number in unit:
                if number < tiles:
                    here = x_ref[part, number * LANES : (number + 1) * LANES]
                    moved = pltpu.roll(here, 2, 1)
                    twice = jnp.where(lane < 2, older, moved)
                    even = win_ref[3, part] * here + win_ref[1, part] * twice
                    odd = win_ref[2, part] * here + win_ref[0, part] * twice
                else:
                    moved = nothing
                    twice = jnp.where(lane < 2, older, 0.0)
                    even = win_ref[1, part] * twice
                    odd = win_ref[0, part] * twice
                sum_moved = pltpu.roll(odd, 1, 1)
                filtered = even + jnp.where(lane < 1, sum_older, sum_moved)
                older, sum_older = moved, sum_moved
                for half, value in enumerate(halves(filtered)):
                    row[half].append(value)
            memory[index] = (older, sum_older)
            for half in range(2):
                parts[half].append(jnp.concatenate(row[half], axis=1))
        stack = jnp.concatenate(parts[0] + parts[1], axis=0)
        spectra = jnp.dot(
            w_ref[...], jnp.concatenate([stack, stack], axis=0), preferred_element_type=F32
        )
        for number in unit:
            value = spectra[:, (number - tile) * LANES : (number - tile + 1) * LANES]
            if number == 0:
                own = value
            if number == tiles:
                following = value
                continue
            power = value[:branches] ** 2 + value[branches:] ** 2
            power_ref[:, number * LANES : (number + 1) * LANES] = power
            if number == 0:
                power = jnp.where(lane_index(power.shape) >= edge, power, 0.0)
            total = total + power
    sums = jnp.sum(total, axis=1, keepdims=True)
    sums = jnp.concatenate([sums, jnp.zeros_like(sums)], axis=0)
    lane = lane_index((rows, LANES))
    packed = jnp.where(lane == 2 * edge, sums, 0.0)
    packed = jnp.where(lane < 2 * edge, pltpu.roll(own, edge, 1), packed)
    packed = jnp.where(lane < edge, following, packed)
    packed = jnp.concatenate([packed, jnp.zeros((LANES - rows, LANES), F32)], axis=0)
    packet = jnp.transpose(packed)[:8]
    small_ref[...] = packet
    big_ref[:8] = packet
    big_ref[8:] = power


def channelize(samples, pieces):
    rows, time_count = samples.shape
    branches = rows // 2
    return pl.pallas_call(
        functools.partial(channel_kernel, pieces),
        in_specs=[HBM],
        out_specs=[VM] * 3,
        out_shape=[
            jax.ShapeDtypeStruct((branches, time_count), F32),
            jax.ShapeDtypeStruct((8, LANES), F32),
            jax.ShapeDtypeStruct((8 + branches, LANES), F32),
        ],
        scratch_shapes=[
            pltpu.VMEM((rows, time_count), F32),
            pltpu.VMEM((TAPS, rows, LANES), F32),
            pltpu.VMEM((rows, 4 * rows), BF16),
            pltpu.SemaphoreType.DMA((pieces,)),
        ],
        compiler_params=pltpu.CompilerParams(vmem_limit_bytes=SOURCE_LIMIT),
        name="channelize",
    )(samples)


FINE = 2
PARTS = 3


def trial_rows(selector, trials, value, value_before, products_before):
    joined = jnp.concatenate([value_before, value], axis=1)
    stack = []
    for lag in range(FINE):
        moved = pltpu.roll(joined, lag, 1)[:, LANES:] if lag else value
        stack.extend(thirds(moved))
    products = jnp.dot(selector, jnp.concatenate(stack, axis=0), preferred_element_type=F32)
    rows = products[:trials]
    for step in range(1, LOCAL_MAX // FINE):
        part = slice(step * trials, (step + 1) * trials)
        both = jnp.concatenate([products_before[part], products[part]], axis=1)
        rows = rows + pltpu.roll(both, FINE * step, 1)[:, LANES:]
    width = value.shape[1]
    return rows, value[:, width - LANES :], products[:, width - LANES :]


def first_rows_kernel(peers, time_all, *refs):
    power_ref, packets, selector_ref = refs[0], refs[1 : 1 + peers], refs[1 + peers]
    rows_ref, scale_ref, line_ref, fold_ref = refs[2 + peers :]
    branches = power_ref.shape[0]
    trials = rows_ref.shape[0]
    rank = lax.axis_index("tm")
    edge = TAPS - 1

    line_ref[:8] = jnp.zeros((8, LANES), F32)
    for peer in range(peers):
        spot = pl.multiple_of(((rank ^ peer) + 1) * 8, 8)
        line_ref[pl.ds(spot, 8), :] = packets[peer][:8]
    mine = line_ref[8:]
    amplitude = mine + pltpu.roll(line_ref[: 8 * peers], edge, 0)
    square = amplitude * amplitude
    folded = square + pltpu.roll(square, LANES - branches, 1)
    fold_ref[...] = folded
    kind = row_index(mine.shape) % 8
    whole = jnp.where(kind == 2 * edge, mine, 0.0)
    whole = jnp.where((kind >= edge) & (kind < 2 * edge), folded, whole)
    band_mean = jnp.sum(whole, axis=0, keepdims=True) / time_all
    scale = 1.0 / (band_mean + epsilon)
    firsts = fold_ref[pl.ds(pl.multiple_of(rank * 8, 8), 8), :]
    firsts = jnp.where(row_index(firsts.shape) == 2 * edge, scale, firsts)
    columns = jnp.transpose(firsts)[:branches]
    scale = jnp.broadcast_to(columns[:, 2 * edge : 2 * edge + 1], (branches, LANES))
    scale_ref[...] = scale
    scale = scale[:, :1]

    tail = jnp.zeros((branches, LANES), F32)
    for peer in range(1, peers):
        if peer & (peer + 1) == 0:
            tail = jnp.where((rank ^ (rank - 1)) == peer, packets[peer][8:], tail)
    halo = jnp.where(rank > 0, tail * scale - 1.0, 0.0)
    start = power_ref[:, :LANES]
    for lane in range(edge):
        value = columns[:, edge + lane : edge + lane + 1]
        start = jnp.where(lane_index(start.shape) == lane, value, start)

    selector = selector_ref[...]
    width = rows_ref.shape[1] - LANES
    value = jnp.concatenate([start, power_ref[:, LANES:width]], axis=1) * scale - 1.0
    value = jnp.concatenate([halo, value], axis=1)
    nothing = jnp.zeros((selector.shape[0], LANES), F32)
    rows_ref[...], _, _ = trial_rows(selector, trials, value, jnp.zeros_like(halo), nothing)


def first_rows(power, packets, selector, tiles, time_all):
    branches = power.shape[0]
    trials = selector.shape[0] * FINE // LOCAL_MAX
    peers = len(packets)
    return pl.pallas_call(
        functools.partial(first_rows_kernel, peers, time_all),
        in_specs=[VM] * (2 + peers),
        out_specs=[VM] * 2,
        out_shape=[
            jax.ShapeDtypeStruct((trials, tiles * LANES), F32),
            jax.ShapeDtypeStruct((branches, LANES), F32),
        ],
        scratch_shapes=[
            pltpu.VMEM((8 * (peers + 1), LANES), F32),
            pltpu.VMEM((8 * peers, LANES), F32),
        ],
        compiler_params=PARAMS,
        name="first_rows",
    )(power, *packets, selector)


def more_rows_kernel(start, power_ref, scale_ref, selector_ref, rows_ref):
    trials, width = rows_ref.shape
    scale = scale_ref[:, :1]
    value = power_ref[:, start - LANES : start + width] * scale - 1.0
    selector = selector_ref[...]
    nothing = jnp.zeros((selector.shape[0], LANES), F32)
    rows, _, _ = trial_rows(selector, trials, value, jnp.zeros_like(value[:, :LANES]), nothing)
    rows_ref[...] = rows[:, LANES:]


def more_rows(power, scale, selector, start, tiles):
    trials = selector.shape[0] * FINE // LOCAL_MAX
    return pl.pallas_call(
        functools.partial(more_rows_kernel, start),
        in_specs=[VM] * 3,
        out_specs=VM,
        out_shape=jax.ShapeDtypeStruct((trials, tiles * LANES), F32),
        compiler_params=PARAMS,
        name="more_rows",
    )(power, scale, selector)


def delayed_rows(rows, amount):
    lane = lane_index(amount.shape)
    source = (lane - amount) & (LANES - 1)
    tiles = [
        jnp.take_along_axis(rows[:, start : start + LANES], source, axis=1)
        for start in range(0, rows.shape[1], LANES)
    ]
    moved = [jnp.where(lane < amount, old, new) for old, new in zip(tiles, tiles[1:])]
    return jnp.concatenate(moved, axis=1)


def merged(level, first, refs):
    pick_ref, amount_ref, own_ref, their_ref = refs[:4]
    trials = own_ref.shape[0]
    if first:
        before = jnp.zeros((trials, LANES), F32)
        own = jnp.concatenate([before, own_ref[...]], axis=1)
        their = jnp.concatenate([before, their_ref[...]], axis=1)
    else:
        own = jnp.concatenate([refs[4][:, refs[4].shape[1] - LANES :], own_ref[...]], axis=1)
        their = jnp.concatenate([refs[5][:, refs[5].shape[1] - LANES :], their_ref[...]], axis=1)
    pick = pick_ref[2 * trials * level : 2 * trials * (level + 1)]
    amount = amount_ref[trials * level : trials * (level + 1)]
    stack = jnp.concatenate(thirds(jnp.concatenate([own, their], axis=0)), axis=0)
    picked = jnp.dot(pick, stack, preferred_element_type=F32)
    return picked[:trials, LANES:] + delayed_rows(picked[trials:], amount)


def merge_kernel(level, first, *refs):
    refs[-1][...] = merged(level, first, refs[:-1])


def merge(level, table, own, their, before):
    return pl.pallas_call(
        functools.partial(merge_kernel, level, not before),
        in_specs=[VM] * (4 + len(before)),
        out_specs=VM,
        out_shape=jax.ShapeDtypeStruct(own.shape, F32),
        compiler_params=PARAMS,
        name="merge",
    )(*table, own, their, *before)


def tables_kernel(divisor, width_ref, delay_ref, table_ref, after_ref, *refs):
    del after_ref
    selector_ref, mask_ref, factor_ref, pick_ref, amount_ref = refs
    trials, channels = delay_ref.shape
    depth = FINE * PARTS * channels
    spread = row_index((channels, depth)) == lane_index((channels, depth)) % channels
    wanted = jnp.dot(
        delay_ref[...].astype(BF16), spread.astype(BF16), preferred_element_type=F32
    ).astype(jnp.int32)
    offset = lane_index((trials, depth)) // (PARTS * channels)
    coarse = LOCAL_MAX // FINE
    selector = jnp.concatenate(
        [(wanted == offset + FINE * step).astype(F32) for step in range(coarse)], axis=0
    ).astype(BF16)
    selector_ref[...] = selector

    shape = (2 * LANES, LANES)
    back = lane_index(shape) + LANES - row_index(shape)
    boxes = width_ref.shape[0]
    wide = jnp.ones(factor_ref.shape, jnp.int32)
    for box in range(boxes):
        inside = (back >= 0) & (back < width_ref[box])
        mask_ref[:, box * LANES : (box + 1) * LANES] = inside.astype(F32).astype(BF16)
        wide = jnp.where(row_index(wide.shape) == box, width_ref[box], wide)
    factor_ref[...] = 1.0 / (jnp.sqrt(wide.astype(F32)) * divisor)
    entries = table_ref[...].astype(jnp.int32)
    column = lane_index((trials, 2 * trials))
    for level in range(amount_ref.shape[0] // trials):
        upper = (lax.axis_index("freq") >> level) & 1
        low = entries[:, 3 * level : 3 * level + 1] + upper * trials
        high = entries[:, 3 * level + 1 : 3 * level + 2] + (1 - upper) * trials
        pick = jnp.concatenate([column == low, column == high], axis=0).astype(F32)
        pick = jnp.concatenate([pick] * 3, axis=1).astype(BF16)
        pick_ref[2 * trials * level : 2 * trials * (level + 1)] = pick
        amount = entries[:, 3 * level + 2 : 3 * level + 3]
        amount_ref[trials * level : trials * (level + 1)] = jnp.broadcast_to(amount, (trials, LANES))


def tables(widths, delays, entries, levels, divisor, after):
    boxes = widths.shape[0]
    trials, channels = delays.shape
    return pl.pallas_call(
        functools.partial(tables_kernel, divisor),
        in_specs=[SM, VM, VM, VM],
        out_specs=[VM] * 5,
        out_shape=[
            jax.ShapeDtypeStruct((LOCAL_MAX // FINE * trials, FINE * PARTS * channels), BF16),
            jax.ShapeDtypeStruct((2 * LANES, boxes * LANES), BF16),
            jax.ShapeDtypeStruct((-(-boxes // 8) * 8, LANES), F32),
            jax.ShapeDtypeStruct((2 * trials * levels, 6 * trials), BF16),
            jax.ShapeDtypeStruct((trials * levels, LANES), jnp.int32),
        ],
        compiler_params=PARAMS,
        name="tables",
    )(widths, delays, entries, after)


def boxcar_pieces(rows, mask_ref, factor_ref, out_ref, begin, end):
    boxes, trials, _ = out_ref.shape
    pairs = [rows[:, tile * LANES : (tile + 2) * LANES] for tile in range(begin, end)]
    high, low = halves(jnp.concatenate(pairs, axis=0))
    mask = mask_ref[...]
    sums = jnp.dot(high, mask, preferred_element_type=F32)
    sums = sums + jnp.dot(low, mask, preferred_element_type=F32)
    for box in range(boxes):
        factor = factor_ref[box : box + 1]
        for tile in range(begin, end):
            line = slice((tile - begin) * trials, (tile - begin + 1) * trials)
            value = sums[line, box * LANES : (box + 1) * LANES] * factor
            out_ref[box, :, tile * LANES : (tile + 1) * LANES] = value


def detect_kernel(level, first, *refs):
    mask_ref, factor_ref = refs[2:4]
    rows_ref, out_ref = refs[-2:]
    rows = merged(level, first, (*refs[:2], *refs[4:8]))
    rows_ref[...] = rows
    if not first:
        before = refs[8]
        rows = jnp.concatenate([before[:, before.shape[1] - LANES :], rows], axis=1)
    boxcar_pieces(rows, mask_ref, factor_ref, out_ref, 0, out_ref.shape[2] // LANES)


def detect(level, table, masks, own, their, before):
    trials, width = own.shape
    operands = [*table, *masks, own, their, *before]
    boxes = masks[0].shape[1] // LANES
    if not before:
        width = width - LANES
    return pl.pallas_call(
        functools.partial(detect_kernel, level, not before),
        in_specs=[VM] * len(operands),
        out_specs=[VM] * 2,
        out_shape=[
            jax.ShapeDtypeStruct(own.shape, F32),
            jax.ShapeDtypeStruct((boxes, trials, width), F32),
        ],
        compiler_params=PARAMS,
        name="detect",
    )(*operands)


def finish_kernel(level, *refs):
    mask_ref, factor_ref = refs[2:4]
    before, ready = refs[8], refs[9:-3]
    out_hbm, out_ref, sem = refs[-3:]
    boxes = out_ref.shape[0]
    copies = []

    def write(source, box, begin, end, start):
        number = len(copies)
        copies.append(
            pltpu.make_async_copy(
                source.at[box, :, pl.ds(begin, end - begin)],
                out_hbm.at[:, box, pl.ds(start + begin, end - begin)],
                sem.at[number],
            )
        )
        copies[-1].start()

    start = 0
    for piece in ready:
        for box in range(boxes):
            write(piece, box, 0, piece.shape[2], start)
        start += piece.shape[2]
    rows = merged(level, False, (*refs[:2], *refs[4:8]))
    rows = jnp.concatenate([before[:, before.shape[1] - LANES :], rows], axis=1)
    tiles = out_ref.shape[2] // LANES
    bounds = [tiles * part // OUT_COPIES for part in range(OUT_COPIES + 1)]
    for begin, end in zip(bounds, bounds[1:]):
        boxcar_pieces(rows, mask_ref, factor_ref, out_ref, begin, end)
        for box in range(boxes):
            write(out_ref, box, begin * LANES, end * LANES, start)
    for copy in copies:
        copy.wait()


def finish(level, table, masks, own, their, before, ready):
    trials, width = own.shape
    operands = [*table, *masks, own, their, *before, *ready]
    boxes = masks[0].shape[1] // LANES
    time_count = width + sum(piece.shape[2] for piece in ready)
    return pl.pallas_call(
        functools.partial(finish_kernel, level),
        in_specs=[VM] * len(operands),
        out_specs=HBM,
        out_shape=jax.ShapeDtypeStruct((trials, boxes, time_count), F32),
        scratch_shapes=[
            pltpu.VMEM((boxes, trials, width), F32),
            pltpu.SemaphoreType.DMA((boxes * (len(ready) + OUT_COPIES),)),
        ],
        compiler_params=PARAMS,
        name="finish",
    )(*operands)


def selector_rows(chosen, row_count):
    return (chosen[:, None] == jnp.arange(row_count, dtype=jnp.int32)[None, :]).astype(F32)


def delay_rows(picked_high, delay_amount, delay_reach):
    current = picked_high
    for bit_index in range(delay_reach.bit_length()):
        step_size = 2**bit_index
        moved = jnp.concatenate(
            [
                jnp.zeros((current.shape[0], step_size), F32),
                current[:, : current.shape[1] - step_size],
            ],
            axis=1,
        )
        bit_set = (jnp.right_shift(delay_amount, bit_index) % 2 == 1)[:, None]
        current = jnp.where(bit_set, moved, current)
    return current[:, delay_reach:]


def merge_level(own_rows, their_rows, level_table, is_upper, delay_reach):
    lower_rows = jnp.where(is_upper, their_rows, own_rows)
    upper_rows = jnp.where(is_upper, own_rows, their_rows)
    row_count = own_rows.shape[0]
    pick = functools.partial(jnp.dot, precision=lax.Precision.HIGHEST, preferred_element_type=F32)
    picked_low = pick(selector_rows(level_table[0], row_count), lower_rows[:, delay_reach:])
    picked_high = pick(selector_rows(level_table[1], row_count), upper_rows)
    return picked_low + delay_rows(picked_high, level_table[2], delay_reach)


def boxcar(dedispersed, widths):
    time_count = dedispersed.shape[1] - (WMAX - 1)
    detection = jnp.zeros((dedispersed.shape[0], widths.shape[0], time_count), F32)
    for offset in range(WMAX):
        width_mask = (offset < widths).astype(F32)
        lagged = dedispersed[:, WMAX - 1 - offset : WMAX - 1 - offset + time_count]
        detection = detection + lagged[:, None, :] * width_mask[None, :, None]
    return detection / jnp.sqrt(widths.astype(F32))[None, :, None]


def body(voltages, local_delay, merge_table, box_widths):
    branches = voltages.shape[2]
    time_count = voltages.shape[3]
    freq_size = lax.axis_size("freq")
    tm_size = lax.axis_size("tm")
    level_count = freq_size.bit_length() - 1
    streamed = min(STREAMED, level_count)
    trials = local_delay.shape[0]
    divisor = math.sqrt(branches * freq_size)

    power, small, big = channelize(voltages.reshape(2 * branches, time_count), FETCHES)
    packets = [small]
    for peer in range(1, tm_size):
        packets.append(swapped(big if peer & (peer + 1) == 0 else small, "tm", peer))

    entries = merge_table[:streamed].reshape(3 * streamed, trials).T.astype(F32)
    entries = jnp.pad(entries, ((0, 0), (0, LANES - 3 * streamed)))
    tiles = 1 + time_count // LANES
    sizes = [tiles * share // sum(SHARES) for share in SHARES]
    sizes[-1] += tiles - sum(sizes)
    starts = [sum(sizes[:i]) * LANES - LANES for i in range(len(sizes))]
    selector, mask, factor, *table = tables(
        box_widths, local_delay, entries, streamed, divisor, small
    )
    masks = (mask, factor)
    rows, scale = first_rows(power, packets, selector, sizes[0], float(time_count * tm_size))
    pieces = [rows]
    for i in range(1, PIECES):
        pieces.append(more_rows(power, scale, selector, starts[i], sizes[i]))

    for level in range(streamed):
        their = []
        for piece in pieces:
            their.append(swapped(piece, "freq", 2**level))
        results = []
        ready = []
        for i in range(PIECES):
            before = [pieces[i - 1], their[i - 1]] if i else []
            if level < level_count - 1:
                results.append(merge(level, table, pieces[i], their[i], before))
                continue
            if i:
                before.append(results[i - 1])
            if i == PIECES - 1:
                return finish(level, table, masks, pieces[i], their[i], before, ready)
            rows, boxed = detect(level, table, masks, pieces[i], their[i], before)
            results.append(rows)
            ready.append(boxed)
        pieces = results
    freq_rank = lax.axis_index("freq")
    dm_rows = jnp.concatenate(pieces, axis=1)[:, LANES:]
    for level_index in range(streamed, level_count):
        delay_reach = SHIFT_UNIT * 2**level_index
        tail_rows = shifted(dm_rows[:, time_count - delay_reach :], "tm", 1)
        own_rows = jnp.concatenate([tail_rows, dm_rows], axis=1)
        their_rows = swapped(own_rows, "freq", 2**level_index)
        is_upper = jnp.right_shift(freq_rank, level_index) % 2 == 1
        dm_rows = merge_level(own_rows, their_rows, merge_table[level_index], is_upper, delay_reach)
    tail_rows = shifted(dm_rows[:, time_count - (WMAX - 1) :], "tm", 1)
    return boxcar(jnp.concatenate([tail_rows, dm_rows], axis=1) / divisor, box_widths)


def solution(mesh):
    return jax.shard_map(
        body,
        mesh=mesh,
        in_specs=(P("freq", None, None, "tm"), P("freq", None), P(None, None, "freq"), P()),
        out_specs=P("freq", None, "tm"),
        check_vma=False,
    )
```

```python
import functools
import math

import jax
import jax.numpy as jnp
from jax import lax
from jax.experimental import pallas as pl
from jax.experimental.pallas import tpu as pltpu
from jax.sharding import PartitionSpec as P

TAPS = 4
LOCAL_MAX = 16
SHIFT_UNIT = 8
WMAX = 32
LANES = 128
OUT_COPIES = 2
ROW_TILES = 8
FETCHES = 1
UNIT = 2
SHARES = (19, 8, 6)
PIECES = len(SHARES)
STREAMED = 3

epsilon = 1e-06

VM = pl.BlockSpec(memory_space=pltpu.VMEM)
SM = pl.BlockSpec(memory_space=pltpu.SMEM)
HBM = pl.BlockSpec(memory_space=pltpu.HBM)
PARAMS = pltpu.CompilerParams(vmem_limit_bytes=16 << 20)
SOURCE_LIMIT = 55_500_000
F32 = jnp.float32
BF16 = jnp.bfloat16


def swapped(value, axis, mask):
    pairs = [(source, source ^ mask) for source in range(lax.axis_size(axis))]
    return lax.ppermute(value, axis, pairs)


def shifted(block, axis, distance):
    devices = range(lax.axis_size(axis))
    route = [(i - distance, i) for i in devices if i - distance in devices]
    return lax.ppermute(block, axis, route)


def window_columns(branches):
    shape = (branches, LANES)
    place = (lane_index(shape) % TAPS * branches + row_index(shape)).astype(F32)
    length = TAPS * branches
    offset = (place - length / 2 + 0.5) * (math.pi / branches)
    hamming = 0.54 - 0.46 * jnp.cos(place * (2.0 * math.pi / (length - 1)))
    return jnp.sin(offset) / offset * hamming


def fourier_rows(branches):
    shape = (2 * branches, 4 * branches)
    row, column = row_index(shape), lane_index(shape)
    quarter = branches // 4
    turn = (row % branches) * (column % branches)
    turn = turn + jnp.where(row >= branches, 2 * quarter, quarter)
    turn = turn - jnp.where(column % (2 * branches) >= branches, quarter, 0)
    turn = turn % branches
    negative = turn > 2 * quarter
    turn = jnp.where(negative, turn - 2 * quarter, turn)
    turn = jnp.where(turn > quarter, 2 * quarter - turn, turn)
    value = jnp.zeros(shape, F32)
    for step in range(1, quarter + 1):
        value = jnp.where(turn == step, math.sin(2.0 * math.pi * step / branches), value)
    return jnp.where(negative, -value, value)


def halves(x):
    high = x.astype(BF16)
    return high, (x - high.astype(F32)).astype(BF16)


def thirds(x):
    high = x.astype(BF16)
    rest = x - high.astype(F32)
    middle = rest.astype(BF16)
    return high, middle, (rest - middle.astype(F32)).astype(BF16)


def lane_index(shape):
    return lax.broadcasted_iota(jnp.int32, shape, len(shape) - 1)


def row_index(shape):
    return lax.broadcasted_iota(jnp.int32, shape, 0)


def channel_kernel(
    pieces, x_hbm, power_ref, small_ref, big_ref, x_ref, win_ref, w_ref, sems
):
    rows, time_count = x_ref.shape
    branches = rows // 2
    width = time_count // pieces
    edge = TAPS - 1
    copies = []
    for piece in range(pieces):
        part = pl.ds(piece * width, width)
        copies.append(pltpu.make_async_copy(x_hbm.at[:, part], x_ref.at[:, part], sems.at[piece]))
        copies[-1].start()
    window = window_columns(branches)
    for tap in range(TAPS):
        column = jnp.broadcast_to(window[:, tap : tap + 1], (branches, LANES))
        win_ref[tap, :branches] = column
        win_ref[tap, branches:] = column
    w_ref[...] = jnp.concatenate(halves(fourier_rows(branches)), axis=1)

    group = 16
    lane = lane_index((group, LANES))
    nothing = jnp.zeros((group, LANES), F32)
    memory = [(nothing, nothing)] * (rows // group)
    total = jnp.zeros((branches, LANES), F32)
    tiles = time_count // LANES
    for tile in range(0, tiles + 1, UNIT):
        if tile < tiles and tile * LANES % width == 0:
            copies[tile * LANES // width].wait()
        unit = range(tile, min(tile + UNIT, tiles + 1))
        parts = {0: [], 1: []}
        for index in range(rows // group):
            part = slice(index * group, (index + 1) * group)
            older, sum_older = memory[index]
            row = {0: [], 1: []}
            for number in unit:
                if number < tiles:
                    here = x_ref[part, number * LANES : (number + 1) * LANES]
                    moved = pltpu.roll(here, 2, 1)
                    twice = jnp.where(lane < 2, older, moved)
                    even = win_ref[3, part] * here + win_ref[1, part] * twice
                    odd = win_ref[2, part] * here + win_ref[0, part] * twice
                else:
                    moved = nothing
                    twice = jnp.where(lane < 2, older, 0.0)
                    even = win_ref[1, part] * twice
                    odd = win_ref[0, part] * twice
                sum_moved = pltpu.roll(odd, 1, 1)
                filtered = even + jnp.where(lane < 1, sum_older, sum_moved)
                older, sum_older = moved, sum_moved
                for half, value in enumerate(halves(filtered)):
                    row[half].append(value)
            memory[index] = (older, sum_older)
            for half in range(2):
                parts[half].append(jnp.concatenate(row[half], axis=1))
        stack = jnp.concatenate(parts[0] + parts[1], axis=0)
        spectra = jnp.dot(
            w_ref[...], jnp.concatenate([stack, stack], axis=0), preferred_element_type=F32
        )
        for number in unit:
            value = spectra[:, (number - tile) * LANES : (number - tile + 1) * LANES]
            if number == 0:
                own = value
            if number == tiles:
                following = value
                continue
            power = value[:branches] ** 2 + value[branches:] ** 2
            power_ref[:, number * LANES : (number + 1) * LANES] = power
            if number == 0:
                power = jnp.where(lane_index(power.shape) >= edge, power, 0.0)
            total = total + power
    sums = jnp.sum(total, axis=1, keepdims=True)
    sums = jnp.concatenate([sums, jnp.zeros_like(sums)], axis=0)
    lane = lane_index((rows, LANES))
    packed = jnp.where(lane == 2 * edge, sums, 0.0)
    packed = jnp.where(lane < 2 * edge, pltpu.roll(own, edge, 1), packed)
    packed = jnp.where(lane < edge, following, packed)
    packed = jnp.concatenate([packed, jnp.zeros((LANES - rows, LANES), F32)], axis=0)
    packet = jnp.transpose(packed)[:8]
    small_ref[...] = packet
    big_ref[:8] = packet
    big_ref[8:] = power


def channelize(samples, pieces):
    rows, time_count = samples.shape
    branches = rows // 2
    return pl.pallas_call(
        functools.partial(channel_kernel, pieces),
        in_specs=[HBM],
        out_specs=[VM] * 3,
        out_shape=[
            jax.ShapeDtypeStruct((branches, time_count), F32),
            jax.ShapeDtypeStruct((8, LANES), F32),
            jax.ShapeDtypeStruct((8 + branches, LANES), F32),
        ],
        scratch_shapes=[
            pltpu.VMEM((rows, time_count), F32),
            pltpu.VMEM((TAPS, rows, LANES), F32),
            pltpu.VMEM((rows, 4 * rows), BF16),
            pltpu.SemaphoreType.DMA((pieces,)),
        ],
        compiler_params=pltpu.CompilerParams(vmem_limit_bytes=SOURCE_LIMIT),
        name="channelize",
    )(samples)


FINE = 2
PARTS = 3


def trial_rows(selector, trials, value, value_before, products_before):
    joined = jnp.concatenate([value_before, value], axis=1)
    stack = []
    for lag in range(FINE):
        moved = pltpu.roll(joined, lag, 1)[:, LANES:] if lag else value
        stack.extend(thirds(moved))
    products = jnp.dot(selector, jnp.concatenate(stack, axis=0), preferred_element_type=F32)
    rows = products[:trials]
    for step in range(1, LOCAL_MAX // FINE):
        part = slice(step * trials, (step + 1) * trials)
        both = jnp.concatenate([products_before[part], products[part]], axis=1)
        rows = rows + pltpu.roll(both, FINE * step, 1)[:, LANES:]
    width = value.shape[1]
    return rows, value[:, width - LANES :], products[:, width - LANES :]


def store_rows(selector, value, rows_ref, skip):
    trials = rows_ref.shape[0]
    before = jnp.zeros((value.shape[0], LANES), F32)
    products = jnp.zeros((selector.shape[0], LANES), F32)
    for start in range(0, value.shape[1], ROW_TILES * LANES):
        part = value[:, start : start + ROW_TILES * LANES]
        rows, before, products = trial_rows(selector, trials, part, before, products)
        first = max(skip - start, 0)
        end = start + part.shape[1] - skip
        rows_ref[:, max(start - skip, 0) : end] = rows[:, first:]


def first_rows_kernel(peers, time_all, *refs):
    power_ref, packets, selector_ref = refs[0], refs[1 : 1 + peers], refs[1 + peers]
    rows_ref, scale_ref, line_ref, fold_ref = refs[2 + peers :]
    branches = power_ref.shape[0]
    rank = lax.axis_index("tm")
    edge = TAPS - 1

    line_ref[:8] = jnp.zeros((8, LANES), F32)
    for peer in range(peers):
        spot = pl.multiple_of(((rank ^ peer) + 1) * 8, 8)
        line_ref[pl.ds(spot, 8), :] = packets[peer][:8]
    mine = line_ref[8:]
    amplitude = mine + pltpu.roll(line_ref[: 8 * peers], edge, 0)
    square = amplitude * amplitude
    folded = square + pltpu.roll(square, LANES - branches, 1)
    fold_ref[...] = folded
    kind = row_index(mine.shape) % 8
    whole = jnp.where(kind == 2 * edge, mine, 0.0)
    whole = jnp.where((kind >= edge) & (kind < 2 * edge), folded, whole)
    band_mean = jnp.sum(whole, axis=0, keepdims=True) / time_all
    scale = 1.0 / (band_mean + epsilon)
    firsts = fold_ref[pl.ds(pl.multiple_of(rank * 8, 8), 8), :]
    firsts = jnp.where(row_index(firsts.shape) == 2 * edge, scale, firsts)
    columns = jnp.transpose(firsts)[:branches]
    scale = jnp.broadcast_to(columns[:, 2 * edge : 2 * edge + 1], (branches, LANES))
    scale_ref[...] = scale
    scale = scale[:, :1]

    tail = jnp.zeros((branches, LANES), F32)
    for peer in range(1, peers):
        if peer & (peer + 1) == 0:
            tail = jnp.where((rank ^ (rank - 1)) == peer, packets[peer][8:], tail)
    halo = jnp.where(rank > 0, tail * scale - 1.0, 0.0)
    start = power_ref[:, :LANES]
    for lane in range(edge):
        value = columns[:, edge + lane : edge + lane + 1]
        start = jnp.where(lane_index(start.shape) == lane, value, start)

    selector = selector_ref[...]
    width = rows_ref.shape[1] - LANES
    value = jnp.concatenate([start, power_ref[:, LANES:width]], axis=1) * scale - 1.0
    value = jnp.concatenate([halo, value], axis=1)
    store_rows(selector, value, rows_ref, 0)


def first_rows(power, packets, selector, tiles, time_all):
    branches = power.shape[0]
    trials = selector.shape[0] * FINE // LOCAL_MAX
    peers = len(packets)
    return pl.pallas_call(
        functools.partial(first_rows_kernel, peers, time_all),
        in_specs=[VM] * (2 + peers),
        out_specs=[VM] * 2,
        out_shape=[
            jax.ShapeDtypeStruct((trials, tiles * LANES), F32),
            jax.ShapeDtypeStruct((branches, LANES), F32),
        ],
        scratch_shapes=[
            pltpu.VMEM((8 * (peers + 1), LANES), F32),
            pltpu.VMEM((8 * peers, LANES), F32),
        ],
        compiler_params=PARAMS,
        name="first_rows",
    )(power, *packets, selector)


def more_rows_kernel(start, power_ref, scale_ref, selector_ref, rows_ref):
    width = rows_ref.shape[1]
    scale = scale_ref[:, :1]
    value = power_ref[:, start - LANES : start + width] * scale - 1.0
    store_rows(selector_ref[...], value, rows_ref, LANES)


def more_rows(power, scale, selector, start, tiles):
    trials = selector.shape[0] * FINE // LOCAL_MAX
    return pl.pallas_call(
        functools.partial(more_rows_kernel, start),
        in_specs=[VM] * 3,
        out_specs=VM,
        out_shape=jax.ShapeDtypeStruct((trials, tiles * LANES), F32),
        compiler_params=PARAMS,
        name="more_rows",
    )(power, scale, selector)


def delayed_rows(rows, amount):
    lane = lane_index(amount.shape)
    source = (lane - amount) & (LANES - 1)
    tiles = [
        jnp.take_along_axis(rows[:, start : start + LANES], source, axis=1)
        for start in range(0, rows.shape[1], LANES)
    ]
    moved = [jnp.where(lane < amount, old, new) for old, new in zip(tiles, tiles[1:])]
    return jnp.concatenate(moved, axis=1)


def merged(level, first, refs):
    pick_ref, amount_ref, own_ref, their_ref = refs[:4]
    trials = own_ref.shape[0]
    if first:
        before = jnp.zeros((trials, LANES), F32)
        own = jnp.concatenate([before, own_ref[...]], axis=1)
        their = jnp.concatenate([before, their_ref[...]], axis=1)
    else:
        own = jnp.concatenate([refs[4][:, refs[4].shape[1] - LANES :], own_ref[...]], axis=1)
        their = jnp.concatenate([refs[5][:, refs[5].shape[1] - LANES :], their_ref[...]], axis=1)
    pick = pick_ref[2 * trials * level : 2 * trials * (level + 1)]
    amount = amount_ref[trials * level : trials * (level + 1)]
    stack = jnp.concatenate(thirds(jnp.concatenate([own, their], axis=0)), axis=0)
    picked = jnp.dot(pick, stack, preferred_element_type=F32)
    return picked[:trials, LANES:] + delayed_rows(picked[trials:], amount)


def merge_kernel(level, first, *refs):
    refs[-1][...] = merged(level, first, refs[:-1])


def merge(level, table, own, their, before):
    return pl.pallas_call(
        functools.partial(merge_kernel, level, not before),
        in_specs=[VM] * (4 + len(before)),
        out_specs=VM,
        out_shape=jax.ShapeDtypeStruct(own.shape, F32),
        compiler_params=PARAMS,
        name="merge",
    )(*table, own, their, *before)


def tables_kernel(divisor, width_ref, delay_ref, table_ref, after_ref, *refs):
    del after_ref
    selector_ref, mask_ref, factor_ref, pick_ref, amount_ref = refs
    trials, channels = delay_ref.shape
    depth = FINE * PARTS * channels
    spread = row_index((channels, depth)) == lane_index((channels, depth)) % channels
    wanted = jnp.dot(
        delay_ref[...].astype(BF16), spread.astype(BF16), preferred_element_type=F32
    ).astype(jnp.int32)
    offset = lane_index((trials, depth)) // (PARTS * channels)
    coarse = LOCAL_MAX // FINE
    selector = jnp.concatenate(
        [(wanted == offset + FINE * step).astype(F32) for step in range(coarse)], axis=0
    ).astype(BF16)
    selector_ref[...] = selector

    shape = (2 * LANES, LANES)
    back = lane_index(shape) + LANES - row_index(shape)
    boxes = width_ref.shape[0]
    wide = jnp.ones(factor_ref.shape, jnp.int32)
    for box in range(boxes):
        inside = (back >= 0) & (back < width_ref[box])
        mask_ref[:, box * LANES : (box + 1) * LANES] = inside.astype(F32).astype(BF16)
        wide = jnp.where(row_index(wide.shape) == box, width_ref[box], wide)
    factor_ref[...] = 1.0 / (jnp.sqrt(wide.astype(F32)) * divisor)
    entries = table_ref[...].astype(jnp.int32)
    column = lane_index((trials, 2 * trials))
    for level in range(amount_ref.shape[0] // trials):
        upper = (lax.axis_index("freq") >> level) & 1
        low = entries[:, 3 * level : 3 * level + 1] + upper * trials
        high = entries[:, 3 * level + 1 : 3 * level + 2] + (1 - upper) * trials
        pick = jnp.concatenate([column == low, column == high], axis=0).astype(F32)
        pick = jnp.concatenate([pick] * 3, axis=1).astype(BF16)
        pick_ref[2 * trials * level : 2 * trials * (level + 1)] = pick
        amount = entries[:, 3 * level + 2 : 3 * level + 3]
        amount_ref[trials * level : trials * (level + 1)] = jnp.broadcast_to(amount, (trials, LANES))


def tables(widths, delays, entries, levels, divisor, after):
    boxes = widths.shape[0]
    trials, channels = delays.shape
    return pl.pallas_call(
        functools.partial(tables_kernel, divisor),
        in_specs=[SM, VM, VM, VM],
        out_specs=[VM] * 5,
        out_shape=[
            jax.ShapeDtypeStruct((LOCAL_MAX // FINE * trials, FINE * PARTS * channels), BF16),
            jax.ShapeDtypeStruct((2 * LANES, boxes * LANES), BF16),
            jax.ShapeDtypeStruct((-(-boxes // 8) * 8, LANES), F32),
            jax.ShapeDtypeStruct((2 * trials * levels, 6 * trials), BF16),
            jax.ShapeDtypeStruct((trials * levels, LANES), jnp.int32),
        ],
        compiler_params=PARAMS,
        name="tables",
    )(widths, delays, entries, after)


def boxcar_pieces(rows, mask_ref, factor_ref, out_ref, begin, end):
    boxes, trials, _ = out_ref.shape
    pairs = [rows[:, tile * LANES : (tile + 2) * LANES] for tile in range(begin, end)]
    high, low = halves(jnp.concatenate(pairs, axis=0))
    mask = mask_ref[...]
    sums = jnp.dot(high, mask, preferred_element_type=F32)
    sums = sums + jnp.dot(low, mask, preferred_element_type=F32)
    for box in range(boxes):
        factor = factor_ref[box : box + 1]
        for tile in range(begin, end):
            line = slice((tile - begin) * trials, (tile - begin + 1) * trials)
            value = sums[line, box * LANES : (box + 1) * LANES] * factor
            out_ref[box, :, tile * LANES : (tile + 1) * LANES] = value


def detect_kernel(level, first, *refs):
    mask_ref, factor_ref = refs[2:4]
    rows_ref, out_ref = refs[-2:]
    rows = merged(level, first, (*refs[:2], *refs[4:8]))
    rows_ref[...] = rows
    if not first:
        before = refs[8]
        rows = jnp.concatenate([before[:, before.shape[1] - LANES :], rows], axis=1)
    boxcar_pieces(rows, mask_ref, factor_ref, out_ref, 0, out_ref.shape[2] // LANES)


def detect(level, table, masks, own, their, before):
    trials, width = own.shape
    operands = [*table, *masks, own, their, *before]
    boxes = masks[0].shape[1] // LANES
    if not before:
        width = width - LANES
    return pl.pallas_call(
        functools.partial(detect_kernel, level, not before),
        in_specs=[VM] * len(operands),
        out_specs=[VM] * 2,
        out_shape=[
            jax.ShapeDtypeStruct(own.shape, F32),
            jax.ShapeDtypeStruct((boxes, trials, width), F32),
        ],
        compiler_params=PARAMS,
        name="detect",
    )(*operands)


def finish_kernel(level, *refs):
    mask_ref, factor_ref = refs[2:4]
    before, ready = refs[8], refs[9:-3]
    out_hbm, out_ref, sem = refs[-3:]
    boxes = out_ref.shape[0]
    copies = []

    def write(source, box, begin, end, start):
        number = len(copies)
        copies.append(
            pltpu.make_async_copy(
                source.at[box, :, pl.ds(begin, end - begin)],
                out_hbm.at[:, box, pl.ds(start + begin, end - begin)],
                sem.at[number],
            )
        )
        copies[-1].start()

    start = 0
    for piece in ready:
        for box in range(boxes):
            write(piece, box, 0, piece.shape[2], start)
        start += piece.shape[2]
    rows = merged(level, False, (*refs[:2], *refs[4:8]))
    rows = jnp.concatenate([before[:, before.shape[1] - LANES :], rows], axis=1)
    tiles = out_ref.shape[2] // LANES
    bounds = [tiles * part // OUT_COPIES for part in range(OUT_COPIES + 1)]
    for begin, end in zip(bounds, bounds[1:]):
        boxcar_pieces(rows, mask_ref, factor_ref, out_ref, begin, end)
        for box in range(boxes):
            write(out_ref, box, begin * LANES, end * LANES, start)
    for copy in copies:
        copy.wait()


def finish(level, table, masks, own, their, before, ready):
    trials, width = own.shape
    operands = [*table, *masks, own, their, *before, *ready]
    boxes = masks[0].shape[1] // LANES
    time_count = width + sum(piece.shape[2] for piece in ready)
    return pl.pallas_call(
        functools.partial(finish_kernel, level),
        in_specs=[VM] * len(operands),
        out_specs=HBM,
        out_shape=jax.ShapeDtypeStruct((trials, boxes, time_count), F32),
        scratch_shapes=[
            pltpu.VMEM((boxes, trials, width), F32),
            pltpu.SemaphoreType.DMA((boxes * (len(ready) + OUT_COPIES),)),
        ],
        compiler_params=PARAMS,
        name="finish",
    )(*operands)


def selector_rows(chosen, row_count):
    return (chosen[:, None] == jnp.arange(row_count, dtype=jnp.int32)[None, :]).astype(F32)


def delay_rows(picked_high, delay_amount, delay_reach):
    current = picked_high
    for bit_index in range(delay_reach.bit_length()):
        step_size = 2**bit_index
        moved = jnp.concatenate(
            [
                jnp.zeros((current.shape[0], step_size), F32),
                current[:, : current.shape[1] - step_size],
            ],
            axis=1,
        )
        bit_set = (jnp.right_shift(delay_amount, bit_index) % 2 == 1)[:, None]
        current = jnp.where(bit_set, moved, current)
    return current[:, delay_reach:]


def merge_level(own_rows, their_rows, level_table, is_upper, delay_reach):
    lower_rows = jnp.where(is_upper, their_rows, own_rows)
    upper_rows = jnp.where(is_upper, own_rows, their_rows)
    row_count = own_rows.shape[0]
    pick = functools.partial(jnp.dot, precision=lax.Precision.HIGHEST, preferred_element_type=F32)
    picked_low = pick(selector_rows(level_table[0], row_count), lower_rows[:, delay_reach:])
    picked_high = pick(selector_rows(level_table[1], row_count), upper_rows)
    return picked_low + delay_rows(picked_high, level_table[2], delay_reach)


def boxcar(dedispersed, widths):
    time_count = dedispersed.shape[1] - (WMAX - 1)
    detection = jnp.zeros((dedispersed.shape[0], widths.shape[0], time_count), F32)
    for offset in range(WMAX):
        width_mask = (offset < widths).astype(F32)
        lagged = dedispersed[:, WMAX - 1 - offset : WMAX - 1 - offset + time_count]
        detection = detection + lagged[:, None, :] * width_mask[None, :, None]
    return detection / jnp.sqrt(widths.astype(F32))[None, :, None]


def body(voltages, local_delay, merge_table, box_widths):
    branches = voltages.shape[2]
    time_count = voltages.shape[3]
    freq_size = lax.axis_size("freq")
    tm_size = lax.axis_size("tm")
    level_count = freq_size.bit_length() - 1
    streamed = min(STREAMED, level_count)
    trials = local_delay.shape[0]
    divisor = math.sqrt(branches * freq_size)

    power, small, big = channelize(voltages.reshape(2 * branches, time_count), FETCHES)
    packets = [small]
    for peer in range(1, tm_size):
        packets.append(swapped(big if peer & (peer + 1) == 0 else small, "tm", peer))

    entries = merge_table[:streamed].reshape(3 * streamed, trials).T.astype(F32)
    entries = jnp.pad(entries, ((0, 0), (0, LANES - 3 * streamed)))
    tiles = 1 + time_count // LANES
    sizes = [tiles * share // sum(SHARES) for share in SHARES]
    sizes[-1] += tiles - sum(sizes)
    starts = [sum(sizes[:i]) * LANES - LANES for i in range(len(sizes))]
    selector, mask, factor, *table = tables(
        box_widths, local_delay, entries, streamed, divisor, small
    )
    masks = (mask, factor)
    rows, scale = first_rows(power, packets, selector, sizes[0], float(time_count * tm_size))
    pieces = [rows]
    for i in range(1, PIECES):
        pieces.append(more_rows(power, scale, selector, starts[i], sizes[i]))

    for level in range(streamed):
        their = []
        for piece in pieces:
            their.append(swapped(piece, "freq", 2**level))
        results = []
        ready = []
        for i in range(PIECES):
            before = [pieces[i - 1], their[i - 1]] if i else []
            if level < level_count - 1:
                results.append(merge(level, table, pieces[i], their[i], before))
                continue
            if i:
                before.append(results[i - 1])
            if i == PIECES - 1:
                return finish(level, table, masks, pieces[i], their[i], before, ready)
            rows, boxed = detect(level, table, masks, pieces[i], their[i], before)
            results.append(rows)
            ready.append(boxed)
        pieces = results
    freq_rank = lax.axis_index("freq")
    dm_rows = jnp.concatenate(pieces, axis=1)[:, LANES:]
    for level_index in range(streamed, level_count):
        delay_reach = SHIFT_UNIT * 2**level_index
        tail_rows = shifted(dm_rows[:, time_count - delay_reach :], "tm", 1)
        own_rows = jnp.concatenate([tail_rows, dm_rows], axis=1)
        their_rows = swapped(own_rows, "freq", 2**level_index)
        is_upper = jnp.right_shift(freq_rank, level_index) % 2 == 1
        dm_rows = merge_level(own_rows, their_rows, merge_table[level_index], is_upper, delay_reach)
    tail_rows = shifted(dm_rows[:, time_count - (WMAX - 1) :], "tm", 1)
    return boxcar(jnp.concatenate([tail_rows, dm_rows], axis=1) / divisor, box_widths)


def solution(mesh):
    return jax.shard_map(
        body,
        mesh=mesh,
        in_specs=(P("freq", None, None, "tm"), P("freq", None), P(None, None, "freq"), P()),
        out_specs=P("freq", None, "tm"),
        check_vma=False,
    )
```
